128 devices in a mesh: dp: 8 (over z, core), table: 16 (over x, y).
Axes of the slice: x: 4, y: 4, z: 4, core: 2. Of those that a mesh axis runs over, the one named last changes fastest.
Arguments:
- table: bfloat16 [65536, 512], P('table'), may hold values from -6 to 6
- w_in: bfloat16 [512, 2048], replicated, may hold values from -0.25 to 0.25
- w_out: bfloat16 [512, 512], replicated, may hold values from -0.25 to 0.25
- owner: int32 [131072, 2], P(('dp', 'table')), may hold values from 0 to 15, all different within a row; in each aligned block of 1024 rows (0 to 1023, 1024 to 2047, ...) at most 256 rows name the same one
- local_row: int32 [131072, 2], P(('dp', 'table')), may hold values from 0 to 4095
- doc_ids: int32 [128, 1024], P(('dp', 'table')), may hold values from 0 to 3, never falling along the last dimension, each value on 1 to 768 neighbouring positions
- out_grad: bfloat16 [131072, 512], P(('dp', 'table')), may hold values from -6 to 6
Outputs:
- layer_out: bfloat16 [131072, 512], P(('dp', 'table'))
- grad_w_in: float32 [512, 2048], replicated
- grad_w_out: float32 [512, 512], replicated
- grad_table: float32 [65536, 512], P('table', 'dp')
The draws below stay inside these ranges and needn't reach their ends.
Inputs may be any that keep to these rules, and one draw needn't show every extreme that they name: The 2 owners of one event differ; among the events of one block of 1024, no owner is named by more than 256 lookups. `doc_ids`: along a row the ids never fall; every id of 0 to 3 covers 1 to 768 events.
All inputs are finite; a program needn't handle non-finite values.
Results may differ from the reference program's by a relative error of at most 0.014.
Values may be sent and summed in bfloat16 or wider, within the bound.
No kernel may reach another device: no remote copies, remote signals or barrier semaphores. Data moves between devices by JAX's collectives and lax.ppermute only.
A program may use at most 128 MiB of HBM per device.

```python
import math
import jax
import jax.numpy as jnp
import numpy as np
from jax import lax

D = 512
HEADS = 4
NTAB = 2
TOK_DEV = 1024
SEQ_DEV = 4
MAXLEN = 768
ROWS_DEV = 4096
CAP = 256
ROWS = 65536
NBLOCK = 128
TOKENS = 131072
N_TABLE = 16


def with_ends(entries, key, least, largest):
    shape = entries.shape
    place = [jax.random.randint(jax.random.fold_in(key, axis), (), 0, shape[axis]) for axis in range(len(shape))]
    entries = entries.at[tuple(place)].set(least)
    longest = shape.index(max(shape))
    place[longest] = (place[longest] + 1) % shape[longest]
    return entries.at[tuple(place)].set(largest)


def shard_levels(stream_key, dims, pieces, least, largest):
    def one(axis_at, parts):
        steps = jax.random.uniform(jax.random.fold_in(jax.random.fold_in(stream_key, 6), axis_at), (parts,), jnp.float32, least / len(pieces), largest / len(pieces))
        return jnp.repeat(jnp.exp(steps), dims[axis_at] // parts).reshape((-1,) + (1,) * (len(dims) - axis_at - 1))

    factor_of = one(*pieces[0])
    for cut in pieces[1:]:
        factor_of = factor_of * one(*cut)
    return factor_of


def profile(amount, total, reach, skew):
    portions = [(1 << 20) // math.isqrt(rank ** skew) + 1 for rank in range(2, amount + 1)]
    rest, given = total - reach - (amount - 1), [1] * (amount - 1)
    while rest > 0:
        movable = [i for i in range(amount - 1) if given[i] < reach]
        whole, remaining = sum([portions[i] for i in movable]), rest
        for i in movable:
            extra = min(reach - given[i], max(1, remaining * portions[i] // whole), rest)
            given[i] = given[i] + extra
            rest = rest - extra
    return np.array([reach] + given)


def ragged_sizes(key, number_of, total, limit, skew):
    if number_of == 2:
        one = jax.random.randint(key, (), max(1, total - limit), min(limit, total - 1) + 1)
        return jnp.stack([one, total - one])
    sizes = jnp.asarray(profile(number_of, total, limit, skew), jnp.int32)
    twos = (number_of - 1) // 2
    giver, receiver = sizes[1:1 + 2 * twos:2], sizes[2:2 + 2 * twos:2]
    slack = jnp.minimum(giver - 1, limit - receiver)
    shifted = jax.random.randint(jax.random.fold_in(key, 1), (twos,), 0, 1 << 20) % (slack + 1)
    sizes = sizes.at[1:1 + 2 * twos:2].set(giver - shifted).at[2:2 + 2 * twos:2].set(receiver + shifted)
    return sizes[jax.random.permutation(jax.random.fold_in(key, 2), number_of)]


def shared_out(key, own, number, rows, number_of, top, reach, lean):
    sequence = jax.random.permutation(key, number_of)
    crowded, ordinary = portions_of(number_of, rows * top, reach, lean, True), portions_of(number_of, rows * top, reach, lean, False)
    places = jnp.arange(number_of)

    def named(sizes, turn):
        used = int((sizes > 0).sum())
        fixed = max(1, used // 4)
        moved = fixed + (places - fixed + turn * (used - fixed)) % max(1, number_of - fixed)
        return jnp.zeros((number_of,), jnp.int32).at[sequence[jnp.where(places < fixed, places, moved)]].set(jnp.asarray(sizes, jnp.int32))

    sizes = jnp.where(number % 4 == 0, named(crowded, number // 4), named(ordinary, number - number // 4 - 1))
    mixed = jax.random.permutation(jax.random.fold_in(own, 3), number_of)
    giver, sink = mixed[0:number_of // 2 * 2:2], mixed[1:number_of // 2 * 2:2]
    slack = jnp.minimum(sizes[giver] - 1, reach - sizes[sink]) // 2
    slack = jnp.where((giver == sequence[0]) | (sink == sequence[0]) | (sizes[sink] == 0), 0, jnp.maximum(slack, 0))
    moved = jax.random.randint(jax.random.fold_in(own, 4), (number_of // 2,), 0, 1 << 20) % (slack + 1)
    sizes = sizes.at[giver].add(-moved).at[sink].add(moved)
    labels = jnp.searchsorted(jnp.cumsum(sizes), jnp.arange(rows * top), side="right").astype(jnp.int32)
    listing = labels.reshape(top, rows).T
    listing = listing[jax.random.permutation(jax.random.fold_in(own, 1), rows)]
    turn = jax.random.randint(jax.random.fold_in(own, 2), (rows, 1), 0, top)
    return jnp.take_along_axis(listing, (jnp.arange(top)[None, :] + turn) % top, axis=1)


def portions_of(number_of, total, reach, lean, full):
    weights = [(1 << 20) // math.isqrt(grade ** lean) + 1 for grade in range(1, number_of + 1)]
    largest = reach if full else min(reach, max(-(-total // number_of), total * weights[0] // sum(weights)))
    least = 1 if total - largest >= number_of - 1 else 0
    counts, rest = [largest] + [least] * (number_of - 1), total - largest - least * (number_of - 1)
    while rest > 0:
        free = [i for i in range(1, number_of) if counts[i] < largest] or [i for i in range(1, number_of) if counts[i] < reach]
        mass, budget = sum([weights[i] for i in free]), rest
        for i in free:
            extra = min(reach - counts[i], max(1, budget * weights[i] // mass), rest)
            counts[i] = counts[i] + extra
            rest = rest - extra
    return np.array(counts)


def noise(rng, dims, scale, bound, pieces=(), dtype=jnp.bfloat16):
    array = scale * jax.random.normal(rng, dims, jnp.float32)
    if pieces:
        array = array * shard_levels(rng, dims, pieces, -0.22, 0.18)
    return jnp.clip(array, -bound, bound).astype(dtype)


def setup_inputs(seed: int = 0) -> dict:
    seeds = jax.random.split(jax.random.key(seed), 8)
    table = noise(seeds[0], (ROWS, D), 1.0, 6.0, ((0, 16),))
    w_in = noise(seeds[1], (D, 4 * D), D ** -0.5, 0.25)
    w_out = noise(seeds[2], (D, D), D ** -0.5, 0.25)
    owner_keys = jax.random.split(jax.random.fold_in(seeds[3], 1), TOKENS // TOK_DEV)
    owner_turns = jax.random.permutation(jax.random.fold_in(seeds[3], 3), TOKENS // TOK_DEV)
    owner = jax.vmap(lambda own, number: shared_out(jax.random.fold_in(seeds[3], 2), own, number, TOK_DEV, N_TABLE, NTAB, CAP, 2))(owner_keys, owner_turns).reshape((TOKENS, NTAB))
    local_row = with_ends(jax.random.randint(seeds[4], (TOKENS, NTAB), 0, ROWS_DEV), jax.random.fold_in(seeds[4], 1), 0, ROWS_DEV - 1).astype(jnp.int32)
    doc_ids = jax.vmap(lambda own: jnp.searchsorted(jnp.cumsum(ragged_sizes(own, SEQ_DEV, TOK_DEV, MAXLEN, 2)), jnp.arange(TOK_DEV), side="right"))(jax.random.split(seeds[5], NBLOCK)).reshape((NBLOCK, TOK_DEV)).astype(jnp.int32)
    out_grad = noise(seeds[6], (TOKENS, D), 1.0, 6.0, ((0, 128),))
    return {"table": table, "w_in": w_in, "w_out": w_out, "owner": owner, "local_row": local_row, "doc_ids": doc_ids, "out_grad": out_grad}


def normalize(values):
    center = values - lax.optimization_barrier(jnp.mean(values, axis=-1, keepdims=True))
    spread = lax.optimization_barrier(jnp.mean(center * center, axis=-1, keepdims=True))
    return center * lax.rsqrt(spread + 1e-06)

def hstu_layer(inputs, w_in, w_out, segment):
    length, width = inputs.shape
    head_dim = width // HEADS
    widened = inputs.astype(jnp.float32)
    normed = normalize(widened).astype(jnp.bfloat16)
    projected = jax.nn.silu(jnp.dot(normed, w_in, preferred_element_type=jnp.float32)).astype(jnp.bfloat16)
    gate_part, value_part, query_part, key_part = jnp.split(projected, 4, axis=1)
    query_heads = query_part.reshape(length, HEADS, head_dim).astype(jnp.float32)
    key_heads = key_part.reshape(length, HEADS, head_dim).astype(jnp.float32)
    value_heads = value_part.reshape(length, HEADS, head_dim).astype(jnp.float32)
    scores = jnp.einsum('thd,shd->hts', query_heads, key_heads) * head_dim ** (-0.5)
    row_index = lax.broadcasted_iota(jnp.int32, (length, length), 0)
    col_index = lax.broadcasted_iota(jnp.int32, (length, length), 1)
    allowed = (segment[:, None] == segment[None, :]) & (row_index >= col_index)
    weights = (jnp.where(allowed[None], jax.nn.silu(scores), 0.0) / MAXLEN).astype(jnp.bfloat16)
    mixed = jnp.einsum('hts,shd->thd', weights.astype(jnp.float32), value_heads).reshape(length, width)
    gated = (normalize(mixed) * gate_part.astype(jnp.float32)).astype(jnp.bfloat16)
    return (widened + jnp.dot(gated, w_out, preferred_element_type=jnp.float32)).astype(jnp.bfloat16)

def reference(table, w_in, w_out, owner, local_row, doc_ids, out_grad):
    row_ids = (owner * ROWS_DEV + local_row).astype(jnp.int32)
    fetched = jnp.take(table, row_ids.reshape(-1), axis=0).astype(jnp.float32).reshape(TOKENS, NTAB, D)
    embedded = lax.optimization_barrier(jnp.sum(fetched, axis=1)).astype(jnp.bfloat16)
    blocks = embedded.reshape(NBLOCK, TOK_DEV, D)
    cotangents = out_grad.reshape(NBLOCK, TOK_DEV, D)

    def advance(carry, piece):
        block_in, block_seg, block_cot = piece

        def forward(first, second, third):
            return hstu_layer(first, second, third, block_seg)
        result, pullback = jax.vjp(forward, block_in, w_in, w_out)
        grad_embed, grad_first, grad_second = pullback(block_cot)
        return ((carry[0] + grad_first.astype(jnp.float32), carry[1] + grad_second.astype(jnp.float32)), (result, grad_embed))
    start = (jnp.zeros(w_in.shape, jnp.float32), jnp.zeros(w_out.shape, jnp.float32))
    (grad_w_in, grad_w_out), (outputs, embed_grad) = lax.scan(advance, start, (blocks, doc_ids, cotangents))
    per_lookup = jnp.broadcast_to(embed_grad.reshape(TOKENS, 1, D).astype(jnp.float32), (TOKENS, NTAB, D)).reshape(TOKENS * NTAB, D)
    grad_table = jax.ops.segment_sum(per_lookup, row_ids.reshape(-1), num_segments=ROWS)
    return (outputs.reshape(TOKENS, D), grad_w_in, grad_w_out, grad_table)
```

```python
import jax
import jax.numpy as jnp
from jax import lax
from jax.experimental import pallas as pl
from jax.experimental.pallas import tpu as pltpu
from jax.sharding import PartitionSpec as P


HEADS = 4
MAXLEN = 768
EPS = 1e-06
BF = jnp.bfloat16
F32 = jnp.float32
NN = (((1,), (0,)), ((), ()))
NT = (((1,), (1,)), ((), ()))
TN = (((0,), (0,)), ((), ()))


def dot(a, b, dims=NN):
    return lax.dot_general(a, b, dims, preferred_element_type=F32)


def iota(shape, dim):
    return lax.broadcasted_iota(jnp.int32, shape, dim)


def onehot(cond):
    return jnp.where(cond, 1.0, 0.0).astype(BF)


def route_kernel(own_ref, loc_ref, slot_ref, req_ref, *, owners, capacity, dummy):
    own = own_ref[...]
    loc = loc_ref[...]
    rows, lanes = own.shape
    member = jnp.concatenate([onehot(own == o) for o in range(owners)], axis=0)
    total = owners * rows
    upper = onehot(iota((lanes, lanes), 0) <= iota((lanes, lanes), 1))
    inside = dot(member, upper)
    left = iota((total, total), 0)
    right = iota((total, total), 1)
    before = onehot((left // rows == right // rows) & (right < left))
    offset = jnp.sum(dot(before, member), axis=1, keepdims=True)
    place = (inside + offset - 1.0) * member.astype(F32)
    position = place[0:rows]
    for o in range(1, owners):
        position = position + place[o * rows : (o + 1) * rows]
    position = position.astype(jnp.int32)
    slot_ref[...] = own * capacity + position
    who = iota((owners, lanes), 0)
    where = iota((capacity, lanes), 0)
    found = jnp.zeros((3 * owners, capacity), F32)
    for r in range(rows):
        mine = own[r : r + 1, :] == who
        row = loc[r : r + 1, :]
        high = jnp.where(mine, (row >> 8).astype(F32), 0.0).astype(BF)
        low = jnp.where(mine, (row & 255).astype(F32), 0.0).astype(BF)
        left_side = jnp.concatenate([high, low, onehot(mine)], axis=0)
        found = found + dot(left_side, onehot(position[r : r + 1, :] == where), NT)
    high = found[0:owners].astype(jnp.int32)
    low = found[owners : 2 * owners].astype(jnp.int32)
    used = found[2 * owners :] > 0.5
    req_ref[...] = jnp.where(used, high * 256 + low, dummy)


def gather_kernel(ids_ref, table_ref, out_ref, wide, picked):
    step = pl.program_id(0)
    count, width = out_ref.shape
    rows = table_ref.shape[0]
    parts = width // 128
    chunk = 64

    @pl.when(step == 0)
    def _():
        def widen(i, carry):
            base = pl.multiple_of(i * chunk, chunk)
            for c in range(parts):
                wide[pl.ds(base * parts + c, chunk, stride=parts), :] = table_ref[
                    pl.ds(base, chunk), c * 128 : (c + 1) * 128
                ].astype(F32)
            return carry

        lax.fori_loop(0, rows // chunk, widen, 0)
        wide[rows * parts : rows * parts + 8, :] = jnp.zeros((8, 128), F32)

    def copy_rows(k, carry):
        for u in range(16):
            s = k * 16 + u
            row = ids_ref[step * count + s]
            picked[pl.ds(pl.multiple_of(s * parts, parts), parts), :] = wide[
                pl.ds(pl.multiple_of(row * parts, parts), parts), :
            ]
        return carry

    lax.fori_loop(0, count // 16, copy_rows, 0)
    for c in range(parts):
        out_ref[:, c * 128 : (c + 1) * 128] = picked[pl.ds(c, count, stride=parts), :].astype(BF)


def scatter_kernel(ids_ref, cnt_ref, grad_ref, out_ref, even, odd, rows_in):
    step = pl.program_id(0)
    count, width = grad_ref.shape
    parts = width // 128
    rows = out_ref.shape[1]

    @pl.when(step == 0)
    def _():
        def clear(i, carry):
            base = pl.ds(pl.multiple_of(i * 128, 128), 128)
            even[base, :] = jnp.zeros((128, 128), F32)
            odd[base, :] = jnp.zeros((128, 128), F32)
            return carry

        lax.fori_loop(0, rows * parts // 128, clear, 0)

    for c in range(parts):
        rows_in[pl.ds(c, count, stride=parts), :] = grad_ref[:, c * 128 : (c + 1) * 128].astype(F32)

    def add_rows(k, carry):
        for u in range(8):
            s = k * 8 + u
            row = ids_ref[step * count + s]
            total = odd if u % 2 else even
            at = pl.ds(pl.multiple_of(row * parts, parts), parts)
            total[at, :] = (
                total[at, :] + rows_in[pl.ds(pl.multiple_of(s * parts, parts), parts), :]
            )
        return carry

    lax.fori_loop(0, (cnt_ref[step] + 7) // 8, add_rows, 0)

    @pl.when(step == pl.num_programs(0) - 1)
    def _():
        def flush(i, carry):
            for c in range(parts):
                at = pl.ds(i * (128 * parts) + c, 128, stride=parts)
                both = even[at, :] + odd[at, :]
                out_ref[c * 128 : (c + 1) * 128, pl.ds(pl.multiple_of(i * 128, 128), 128)] = (
                    both.T.astype(BF)
                )
            return carry

        lax.fori_loop(0, rows // 128, flush, 0)


def normal(values):
    center = values - jnp.mean(values, axis=-1, keepdims=True)
    spread = jnp.mean(center * center, axis=-1, keepdims=True)
    scale = lax.rsqrt(spread + EPS)
    return center * scale, scale


def normal_back(grad, unit, scale):
    shared = jnp.mean(grad, axis=-1, keepdims=True)
    along = jnp.mean(grad * unit, axis=-1, keepdims=True)
    return scale * (grad - shared - unit * along)


def layer_kernel(
    arrived_ref,
    slot_ref,
    w_in_ref,
    w_out_ref,
    doc_ref,
    og_ref,
    out_ref,
    sending_ref,
    normed_ref,
    du_ref,
    gated_ref,
    emb_ref,
    proj_ref,
    wts_ref,
    dws_ref,
    mixed_ref,
    dmix_ref,
    eg_ref,
):
    events, width = og_ref.shape
    slots = arrived_ref.shape[0]
    head = width // HEADS
    blk = 256
    nblk = events // blk
    lane_rows = events // 128
    cap_step = 256
    slot_all = slot_ref[...]
    slot_cols = slot_all.astype(F32).T.astype(jnp.int32)
    doc_rows = doc_ref[...]
    doc_cols = jnp.broadcast_to(doc_rows.astype(F32), (8, events)).T[:, 0:1].astype(jnp.int32)
    scale = head ** (-0.5)

    for b in range(nblk):
        rows = slice(b * blk, (b + 1) * blk)
        per = blk // 128
        first = jnp.concatenate(
            [slot_cols[:, b * per + i : b * per + i + 1] for i in range(per)], axis=0
        )
        second = jnp.concatenate(
            [slot_cols[:, lane_rows + b * per + i : lane_rows + b * per + i + 1] for i in range(per)],
            axis=0,
        )
        total = jnp.zeros((blk, width), F32)
        for o in range(slots // cap_step):
            where = iota((blk, cap_step), 1) + o * cap_step
            pick = onehot((where == first) | (where == second))
            total = total + dot(pick, arrived_ref[o * cap_step : (o + 1) * cap_step, :])
        embedded = total.astype(BF)
        emb_ref[rows, :] = embedded
        unit, _ = normal(embedded.astype(F32))
        normed = unit.astype(BF)
        normed_ref[rows, :] = normed
        for c in range(4):
            cols = slice(c * width, (c + 1) * width)
            u = dot(normed, w_in_ref[:, cols])
            sig = 0.5 * jnp.tanh(0.5 * u) + 0.5
            act = u * sig
            proj_ref[rows, cols] = act.astype(BF)
            du_ref[rows, cols] = (sig + act * (1.0 - sig)).astype(BF)

    def heads_forward(h, carry):
        def cols(part):
            return pl.ds(pl.multiple_of(part * width + h * head, head), head)

        mine = pl.ds(pl.multiple_of(h * head, head), head)
        for i in range(nblk):
            rows = slice(i * blk, (i + 1) * blk)
            query = proj_ref[rows, cols(2)]
            total = jnp.zeros((blk, head), F32)
            for j in range(i + 1):
                keys = slice(j * blk, (j + 1) * blk)
                scores = dot(query, proj_ref[keys, cols(3)], NT) * scale
                allowed = doc_cols[rows] == doc_rows[:, keys]
                if i == j:
                    allowed = allowed & (iota((blk, blk), 0) >= iota((blk, blk), 1))
                sig = 0.5 * jnp.tanh(0.5 * scores) + 0.5
                act = scores * sig
                weight = jnp.where(allowed, act * (1.0 / MAXLEN), 0.0).astype(BF)
                slope = sig + act * (1.0 - sig)
                wts_ref[h, rows, keys] = weight
                dws_ref[h, rows, keys] = jnp.where(allowed, slope * (scale / MAXLEN), 0.0).astype(BF)
                total = total + dot(weight, proj_ref[keys, cols(1)])
            mixed_ref[rows, mine] = total
        return carry

    lax.fori_loop(0, HEADS, heads_forward, 0)

    for b in range(nblk):
        rows = slice(b * blk, (b + 1) * blk)
        unit, spread = normal(mixed_ref[rows, :])
        gate = proj_ref[rows, 0:width].astype(F32)
        gated = (unit * gate).astype(BF)
        gated_ref[rows, :] = gated
        out_ref[rows, :] = (emb_ref[rows, :].astype(F32) + dot(gated, w_out_ref[...])).astype(BF)
        dgated = dot(og_ref[rows, :], w_out_ref[...], NT).astype(BF).astype(F32)
        dmix_ref[rows, :] = normal_back(dgated * gate, unit, spread).astype(BF)
        dgate = (dgated * unit).astype(BF).astype(F32)
        du_ref[rows, 0:width] = (dgate * du_ref[rows, 0:width].astype(F32)).astype(BF)

    def heads_backward(h, carry):
        def cols(part):
            return pl.ds(pl.multiple_of(part * width + h * head, head), head)

        mine = pl.ds(pl.multiple_of(h * head, head), head)

        def put(rows, part, value):
            at = cols(part)
            du_ref[rows, at] = (
                value.astype(BF).astype(F32) * du_ref[rows, at].astype(F32)
            ).astype(BF)

        for j in range(nblk):
            keys = slice(j * blk, (j + 1) * blk)
            value = proj_ref[keys, cols(1)]
            dkey = jnp.zeros((blk, head), F32)
            dvalue = jnp.zeros((blk, head), F32)
            for i in range(j, nblk):
                rows = slice(i * blk, (i + 1) * blk)
                dmix = dmix_ref[rows, mine]
                dscore = (
                    dot(dmix, value, NT) * dws_ref[h, rows, keys].astype(F32)
                ).astype(BF)
                dws_ref[h, rows, keys] = dscore
                dvalue = dvalue + dot(wts_ref[h, rows, keys], dmix, TN)
                dkey = dkey + dot(dscore, proj_ref[rows, cols(2)], TN)
            put(keys, 1, dvalue)
            put(keys, 3, dkey)
        for i in range(nblk):
            rows = slice(i * blk, (i + 1) * blk)
            upto = slice(0, (i + 1) * blk)
            put(rows, 2, dot(dws_ref[h, rows, upto], proj_ref[upto, cols(3)]))
        return carry

    lax.fori_loop(0, HEADS, heads_backward, 0)

    for b in range(nblk):
        rows = slice(b * blk, (b + 1) * blk)
        dnormed = dot(du_ref[rows, :], w_in_ref[...], NT).astype(BF).astype(F32)
        unit, spread = normal(emb_ref[rows, :].astype(F32))
        grad = normal_back(dnormed, unit, spread) + og_ref[rows, :].astype(F32)
        eg_ref[rows, :] = grad.astype(BF)

    for o in range(slots // cap_step):
        where = iota((cap_step, 128), 0) + o * cap_step
        picks = [
            onehot(
                (where == slot_all[r : r + 1, :])
                | (where == slot_all[lane_rows + r : lane_rows + r + 1, :])
            )
            for r in range(lane_rows)
        ]
        pick = jnp.concatenate(picks, axis=1)
        sending_ref[o * cap_step : (o + 1) * cap_step, :] = dot(pick, eg_ref[...]).astype(BF)


def weights_kernel(normed_ref, du_ref, gated_ref, og_ref, out_ref):
    width = gated_ref.shape[1]
    wide = du_ref.shape[1]
    for c in range(wide // width):
        cols = slice(c * width, (c + 1) * width)
        out_ref[:, cols] = dot(normed_ref[...], du_ref[:, cols], TN).astype(BF)
    out_ref[:, wide:] = dot(gated_ref[...], og_ref[...], TN).astype(BF)


def params(mib, **more):
    return pltpu.CompilerParams(vmem_limit_bytes=mib * 2**20, **more)


def route(own, loc, capacity, owners, dummy):
    return pl.pallas_call(
        lambda *refs: route_kernel(*refs, owners=owners, capacity=capacity, dummy=dummy),
        out_shape=(
            jax.ShapeDtypeStruct(own.shape, jnp.int32),
            jax.ShapeDtypeStruct((owners, capacity), jnp.int32),
        ),
        name="route",
    )(own, loc)


def gather_rows(ids, table, owners, capacity):
    rows, width = table.shape
    parts = width // 128
    return pl.pallas_call(
        gather_kernel,
        out_shape=jax.ShapeDtypeStruct((owners * capacity, width), BF),
        grid_spec=pltpu.PrefetchScalarGridSpec(
            num_scalar_prefetch=1,
            grid=(owners,),
            in_specs=[pl.BlockSpec((rows, width), lambda i, ids: (0, 0))],
            out_specs=pl.BlockSpec((capacity, width), lambda i, ids: (i, 0)),
            scratch_shapes=[
                pltpu.VMEM(((rows + 2) * parts, 128), F32),
                pltpu.VMEM((capacity * parts, 128), F32),
            ],
        ),
        compiler_params=params(32),
        name="gather_rows",
    )(ids, table)


def scatter_rows(ids, counts, grads, rows, owners, capacity):
    width = grads.shape[1]
    parts = width // 128
    return pl.pallas_call(
        scatter_kernel,
        out_shape=jax.ShapeDtypeStruct((width, rows), BF),
        grid_spec=pltpu.PrefetchScalarGridSpec(
            num_scalar_prefetch=2,
            grid=(owners,),
            in_specs=[pl.BlockSpec((capacity, width), lambda i, *_: (i, 0))],
            out_specs=pl.BlockSpec((width, rows), lambda i, *_: (0, 0)),
            scratch_shapes=[
                pltpu.VMEM(((rows + 2) * parts, 128), F32),
                pltpu.VMEM(((rows + 2) * parts, 128), F32),
                pltpu.VMEM((capacity * parts, 128), F32),
            ],
        ),
        compiler_params=params(40),
        name="scatter_rows",
    )(ids, counts, grads)


def layer(arrived, slots, w_in, w_out, doc, og):
    events, width = og.shape
    wide = w_in.shape[1]
    return pl.pallas_call(
        layer_kernel,
        out_shape=(
            jax.ShapeDtypeStruct((events, width), BF),
            jax.ShapeDtypeStruct(arrived.shape, BF),
            jax.ShapeDtypeStruct((events, width), BF),
            jax.ShapeDtypeStruct((events, wide), BF),
            jax.ShapeDtypeStruct((events, width), BF),
        ),
        scratch_shapes=[
            pltpu.VMEM((events, width), BF),
            pltpu.VMEM((events, wide), BF),
            pltpu.VMEM((HEADS, events, events), BF),
            pltpu.VMEM((HEADS, events, events), BF),
            pltpu.VMEM((events, width), F32),
            pltpu.VMEM((events, width), BF),
            pltpu.VMEM((events, width), BF),
        ],
        compiler_params=params(60),
        name="layer",
    )(arrived, slots, w_in, w_out, doc, og)


def weight_grads(normed, du, gated, og):
    width = gated.shape[1]
    return pl.pallas_call(
        weights_kernel,
        out_shape=jax.ShapeDtypeStruct((width, du.shape[1] + width), BF),
        compiler_params=params(32),
        name="weight_grads",
    )(normed, du, gated, og)


def whole(table, w_in, w_out, owner, local_row, doc_ids, out_grad):
    events, lookups_each = owner.shape
    rows_owned, width = table.shape
    owners = lax.axis_size("table")
    lookups = events * lookups_each
    capacity = 2 * lookups // owners
    wide = w_in.shape[1]
    own = owner.T.reshape(lookups // 128, 128)
    loc = local_row.T.reshape(lookups // 128, 128)
    slots, requests = route(own, loc, capacity, owners, rows_owned)
    asked = lax.all_to_all(requests, "table", split_axis=0, concat_axis=0, tiled=True)
    ids = asked.reshape(owners * capacity)
    counts = jnp.sum((asked < rows_owned).astype(jnp.int32), axis=1)
    found = gather_rows(ids, table, owners, capacity).reshape(owners, capacity, width)
    arrived = lax.all_to_all(found, "table", split_axis=0, concat_axis=0, tiled=True)
    layer_out, sending, normed, du, gated = layer(
        arrived.reshape(owners * capacity, width), slots, w_in, w_out, doc_ids, out_grad
    )
    received = lax.all_to_all(
        sending.reshape(owners, capacity, width), "table", split_axis=0, concat_axis=0, tiled=True
    )
    terms = weight_grads(normed, du, gated, out_grad)
    partial = lax.psum_scatter(terms, "dp", scatter_dimension=0, tiled=True)
    partial = lax.psum(partial.astype(F32), "table").astype(BF)
    weights = lax.all_gather(partial, "dp", axis=0, tiled=True).astype(F32)
    summed = scatter_rows(
        ids, counts, received.reshape(owners * capacity, width), rows_owned, owners, capacity
    )
    mine = lax.psum_scatter(summed, "dp", scatter_dimension=0, tiled=True)
    return (layer_out, weights[:, :wide], weights[:, wide:], mine.T.astype(F32))


def solution(mesh):
    placed = (
        P("table", None),
        P(),
        P(),
        P(("dp", "table"), None),
        P(("dp", "table"), None),
        P(("dp", "table"), None),
        P(("dp", "table"), None),
    )
    return jax.shard_map(
        whole,
        mesh=mesh,
        in_specs=placed,
        out_specs=(P(("dp", "table"), None), P(), P(), P("table", "dp")),
        check_vma=False,
    )
```

```python
import jax
import jax.numpy as jnp
from jax import lax
from jax.experimental import pallas as pl
from jax.experimental.pallas import tpu as pltpu
from jax.sharding import PartitionSpec as P


HEADS = 4
MAXLEN = 768
EPS = 1e-06
BF = jnp.bfloat16
F32 = jnp.float32
NN = (((1,), (0,)), ((), ()))
NT = (((1,), (1,)), ((), ()))
TN = (((0,), (0,)), ((), ()))


def dot(a, b, dims=NN):
    return lax.dot_general(a, b, dims, preferred_element_type=F32)


def iota(shape, dim):
    return lax.broadcasted_iota(jnp.int32, shape, dim)


def onehot(cond):
    return jnp.where(cond, 1.0, 0.0).astype(BF)


def route_kernel(own_ref, loc_ref, slot_ref, req_ref, *, owners, capacity, dummy):
    own = own_ref[...]
    loc = loc_ref[...]
    rows, lanes = own.shape
    member = jnp.concatenate([onehot(own == o) for o in range(owners)], axis=0)
    total = owners * rows
    upper = onehot(iota((lanes, lanes), 0) <= iota((lanes, lanes), 1))
    inside = dot(member, upper)
    left = iota((total, total), 0)
    right = iota((total, total), 1)
    before = onehot((left // rows == right // rows) & (right < left))
    offset = jnp.sum(dot(before, member), axis=1, keepdims=True)
    place = (inside + offset - 1.0) * member.astype(F32)
    position = place[0:rows]
    for o in range(1, owners):
        position = position + place[o * rows : (o + 1) * rows]
    position = position.astype(jnp.int32)
    slot_ref[...] = own * capacity + position
    who = iota((owners, lanes), 0)
    where = iota((capacity, lanes), 0)
    found = jnp.zeros((3 * owners, capacity), F32)
    for r in range(rows):
        mine = own[r : r + 1, :] == who
        row = loc[r : r + 1, :]
        high = jnp.where(mine, (row >> 8).astype(F32), 0.0).astype(BF)
        low = jnp.where(mine, (row & 255).astype(F32), 0.0).astype(BF)
        left_side = jnp.concatenate([high, low, onehot(mine)], axis=0)
        found = found + dot(left_side, onehot(position[r : r + 1, :] == where), NT)
    high = found[0:owners].astype(jnp.int32)
    low = found[owners : 2 * owners].astype(jnp.int32)
    used = found[2 * owners :] > 0.5
    req_ref[...] = jnp.where(used, high * 256 + low, dummy)


def gather_kernel(ids_ref, table_ref, out_ref, wide, picked):
    step = pl.program_id(0)
    count, width = out_ref.shape
    rows = table_ref.shape[0]
    parts = width // 128
    chunk = 64

    @pl.when(step == 0)
    def _():
        def widen(i, carry):
            base = pl.multiple_of(i * chunk, chunk)
            for c in range(parts):
                wide[pl.ds(base * parts + c, chunk, stride=parts), :] = table_ref[
                    pl.ds(base, chunk), c * 128 : (c + 1) * 128
                ].astype(F32)
            return carry

        lax.fori_loop(0, rows // chunk, widen, 0)
        wide[rows * parts : rows * parts + 8, :] = jnp.zeros((8, 128), F32)

    def copy_rows(k, carry):
        for u in range(16):
            s = k * 16 + u
            row = ids_ref[step * count + s]
            picked[pl.ds(pl.multiple_of(s * parts, parts), parts), :] = wide[
                pl.ds(pl.multiple_of(row * parts, parts), parts), :
            ]
        return carry

    lax.fori_loop(0, count // 16, copy_rows, 0)
    for c in range(parts):
        out_ref[:, c * 128 : (c + 1) * 128] = picked[pl.ds(c, count, stride=parts), :].astype(BF)


def scatter_kernel(ids_ref, cnt_ref, grad_ref, out_ref, total, rows_in):
    step = pl.program_id(0)
    count, width = grad_ref.shape
    used = width // 128
    rows = out_ref.shape[1]
    parts = rows_in.shape[0] // count

    @pl.when(step == 0)
    def _():
        def clear(i, carry):
            total[pl.ds(pl.multiple_of(i * 256, 256), 256), :] = jnp.zeros((256, 128), F32)
            return carry

        lax.fori_loop(0, rows * parts // 256, clear, 0)

    for c in range(used):
        rows_in[pl.ds(c, count, stride=parts), :] = grad_ref[:, c * 128 : (c + 1) * 128].astype(F32)

    def add_rows(k, carry):
        for u in range(8):
            s = k * 8 + u
            row = ids_ref[step * count + s]
            at = pl.ds(pl.multiple_of(row * parts, parts), parts)
            total[at, :] = (
                total[at, :] + rows_in[pl.ds(pl.multiple_of(s * parts, parts), parts), :]
            )
        return carry

    lax.fori_loop(0, (cnt_ref[step] + 7) // 8, add_rows, 0)

    @pl.when(step == pl.num_programs(0) - 1)
    def _():
        def flush(i, carry):
            for c in range(used):
                block = total[pl.ds(i * (128 * parts) + c, 128, stride=parts), :]
                out_ref[c * 128 : (c + 1) * 128, pl.ds(pl.multiple_of(i * 128, 128), 128)] = (
                    block.T.astype(BF)
                )
            return carry

        lax.fori_loop(0, rows // 128, flush, 0)


def normal(values):
    center = values - jnp.mean(values, axis=-1, keepdims=True)
    spread = jnp.mean(center * center, axis=-1, keepdims=True)
    scale = lax.rsqrt(spread + EPS)
    return center * scale, scale


def normal_back(grad, unit, scale):
    shared = jnp.mean(grad, axis=-1, keepdims=True)
    along = jnp.mean(grad * unit, axis=-1, keepdims=True)
    return scale * (grad - shared - unit * along)


def spread_columns(place_ref, width, shares):
    column = iota((8, width), 1)
    place = place_ref[0]
    source = jnp.zeros((8, width), jnp.int32)
    start = 0
    for share in shares:
        inside = column - 8 * start
        piece = inside // share
        z = (place // 2 + piece) & 3
        core = (place + piece // 4) & 1
        here = (z * 2 + core) * (width // 8) + start + inside - piece * share
        source = jnp.where(inside >= 0, here, source)
        start += share
    return onehot(iota((width, width), 0) == source[0:1, :])


def layer_kernel(
    place_ref,
    arrived_ref,
    slot_ref,
    w_in_ref,
    w_out_ref,
    doc_ref,
    og_ref,
    out_ref,
    send_a_ref,
    send_b_ref,
    normed_ref,
    du_ref,
    gated_ref,
    emb_ref,
    proj_ref,
    wts_ref,
    dws_ref,
    mixed_ref,
    dmix_ref,
    eg_ref,
    col_ref,
):
    events, width = og_ref.shape
    slots = arrived_ref.shape[0]
    head = width // HEADS
    blk = 256
    nblk = events // blk
    lane_rows = events // 128
    cap_step = 256
    slot_all = slot_ref[...]
    slot_cols = slot_all.astype(F32).T.astype(jnp.int32)
    doc_rows = doc_ref[...]
    for r in range(lane_rows):
        rows = slice(r * 128, (r + 1) * 128)
        col_ref[rows, 0:1] = slot_cols[:, r : r + 1]
        col_ref[rows, 1:2] = slot_cols[:, lane_rows + r : lane_rows + r + 1]
    doc_cols = jnp.broadcast_to(doc_rows.astype(F32), (8, events)).T[:, 0:1].astype(jnp.int32)
    col_ref[:, 2:3] = doc_cols
    scale = head ** (-0.5)

    def steps(body, total, group):
        def several(k, carry):
            for u in range(group):
                body(k * group + u, carry)
            return carry

        if total == group:
            several(0, 0)
        else:
            lax.fori_loop(0, total // group, several, 0)

    def block_rows(b):
        return pl.ds(pl.multiple_of(b * blk, blk), blk)

    def unpack(b, carry):
        rows = block_rows(b)
        first = col_ref[rows, 0:1]
        second = col_ref[rows, 1:2]
        total = jnp.zeros((blk, width), F32)
        for o in range(slots // cap_step):
            where = iota((blk, cap_step), 1) + o * cap_step
            pick = onehot((where == first) | (where == second))
            total = total + dot(pick, arrived_ref[o * cap_step : (o + 1) * cap_step, :])
        embedded = total.astype(BF)
        emb_ref[rows, :] = embedded
        unit, _ = normal(embedded.astype(F32))
        normed = unit.astype(BF)
        normed_ref[rows, :] = normed
        for c in range(4):
            cols = slice(c * width, (c + 1) * width)
            u = dot(normed, w_in_ref[:, cols])
            sig = 0.5 * jnp.tanh(0.5 * u) + 0.5
            act = u * sig
            proj_ref[rows, cols] = act.astype(BF)
            du_ref[rows, cols] = (sig + act * (1.0 - sig)).astype(BF)
        return carry

    steps(unpack, nblk, 2)

    def heads_forward(h, carry):
        def cols(part):
            return pl.ds(pl.multiple_of(part * width + h * head, head), head)

        mine = pl.ds(pl.multiple_of(h * head, head), head)
        for i in range(nblk):
            rows = slice(i * blk, (i + 1) * blk)
            query = proj_ref[rows, cols(2)]
            total = jnp.zeros((blk, head), F32)
            for j in range(i + 1):
                keys = slice(j * blk, (j + 1) * blk)
                scores = dot(query, proj_ref[keys, cols(3)], NT) * scale
                allowed = col_ref[rows, 2:3] == doc_rows[:, keys]
                if i == j:
                    allowed = allowed & (iota((blk, blk), 0) >= iota((blk, blk), 1))
                sig = 0.5 * jnp.tanh(0.5 * scores) + 0.5
                act = scores * sig
                weight = jnp.where(allowed, act * (1.0 / MAXLEN), 0.0).astype(BF)
                slope = sig + act * (1.0 - sig)
                wts_ref[h, rows, keys] = weight
                dws_ref[h, rows, keys] = jnp.where(allowed, slope * (scale / MAXLEN), 0.0).astype(BF)
                total = total + dot(weight, proj_ref[keys, cols(1)])
            mixed_ref[rows, mine] = total
        return carry

    lax.fori_loop(0, HEADS, heads_forward, 0)

    def middle(b, carry):
        rows = block_rows(b)
        unit, spread = normal(mixed_ref[rows, :])
        gate = proj_ref[rows, 0:width].astype(F32)
        gated = (unit * gate).astype(BF)
        gated_ref[rows, :] = gated
        out_ref[rows, :] = (emb_ref[rows, :].astype(F32) + dot(gated, w_out_ref[...])).astype(BF)
        dgated = dot(og_ref[rows, :], w_out_ref[...], NT).astype(BF).astype(F32)
        dmix_ref[rows, :] = normal_back(dgated * gate, unit, spread).astype(BF)
        dgate = (dgated * unit).astype(BF).astype(F32)
        du_ref[rows, 0:width] = (dgate * du_ref[rows, 0:width].astype(F32)).astype(BF)
        return carry

    steps(middle, nblk, 1)

    def heads_backward(h, carry):
        def cols(part):
            return pl.ds(pl.multiple_of(part * width + h * head, head), head)

        mine = pl.ds(pl.multiple_of(h * head, head), head)

        def put(rows, part, value):
            at = cols(part)
            du_ref[rows, at] = (
                value.astype(BF).astype(F32) * du_ref[rows, at].astype(F32)
            ).astype(BF)

        for j in range(nblk):
            keys = slice(j * blk, (j + 1) * blk)
            value = proj_ref[keys, cols(1)]
            dkey = jnp.zeros((blk, head), F32)
            dvalue = jnp.zeros((blk, head), F32)
            for i in range(j, nblk):
                rows = slice(i * blk, (i + 1) * blk)
                dmix = dmix_ref[rows, mine]
                dscore = (
                    dot(dmix, value, NT) * dws_ref[h, rows, keys].astype(F32)
                ).astype(BF)
                dws_ref[h, rows, keys] = dscore
                dvalue = dvalue + dot(wts_ref[h, rows, keys], dmix, TN)
                dkey = dkey + dot(dscore, proj_ref[rows, cols(2)], TN)
            put(keys, 1, dvalue)
            put(keys, 3, dkey)
        for i in range(nblk):
            rows = slice(i * blk, (i + 1) * blk)
            upto = slice(0, (i + 1) * blk)
            put(rows, 2, dot(dws_ref[h, rows, upto], proj_ref[upto, cols(3)]))
        return carry

    lax.fori_loop(0, HEADS, heads_backward, 0)

    spread = spread_columns(place_ref, width, (send_a_ref.shape[1] // 8, send_b_ref.shape[1] // 8))

    def last(b, carry):
        rows = block_rows(b)
        dnormed = dot(du_ref[rows, :], w_in_ref[...], NT).astype(BF).astype(F32)
        unit, size = normal(emb_ref[rows, :].astype(F32))
        grad = normal_back(dnormed, unit, size) + og_ref[rows, :].astype(F32)
        eg_ref[rows, :] = dot(grad.astype(BF), spread).astype(BF)
        return carry

    steps(last, nblk, 1)

    def pack(o, carry):
        where = iota((cap_step, 128), 0) + o * cap_step
        picks = [
            onehot(
                (where == slot_all[r : r + 1, :])
                | (where == slot_all[lane_rows + r : lane_rows + r + 1, :])
            )
            for r in range(lane_rows)
        ]
        packed = dot(jnp.concatenate(picks, axis=1), eg_ref[...]).astype(BF)
        at = pl.ds(pl.multiple_of(o * cap_step, cap_step), cap_step)
        send_a_ref[at, :] = packed[:, : send_a_ref.shape[1]]
        send_b_ref[at, :] = packed[:, send_a_ref.shape[1] :]
        return carry

    steps(pack, slots // cap_step, 16)


def weights_kernel(place_ref, normed_ref, du_ref, gated_ref, og_ref, out_ref):
    width = gated_ref.shape[1]
    wide = du_ref.shape[1]
    spread = spread_columns(place_ref, width, (width // 8,))
    normed = dot(normed_ref[...], spread).astype(BF)
    gated = dot(gated_ref[...], spread).astype(BF)

    def columns(c, carry):
        cols = pl.ds(pl.multiple_of(c * width, width), width)
        out_ref[:, cols] = dot(normed, du_ref[:, cols], TN).astype(BF)
        return carry

    lax.fori_loop(0, wide // width, columns, 0)
    out_ref[:, wide:] = dot(gated, og_ref[...], TN).astype(BF)


def finish_kernel(sum_ref, first_ref, second_ref):
    wide = first_ref.shape[1]
    first_ref[...] = sum_ref[:, :wide].astype(F32)
    second_ref[...] = sum_ref[:, wide:].astype(F32)


def params(mib, **more):
    return pltpu.CompilerParams(vmem_limit_bytes=mib * 2**20, **more)


def route(own, loc, capacity, owners, dummy):
    return pl.pallas_call(
        lambda *refs: route_kernel(*refs, owners=owners, capacity=capacity, dummy=dummy),
        out_shape=(
            jax.ShapeDtypeStruct(own.shape, jnp.int32),
            jax.ShapeDtypeStruct((owners, capacity), jnp.int32),
        ),
        name="route",
    )(own, loc)


def finish(summed, wide):
    rows, both = summed.shape
    return pl.pallas_call(
        finish_kernel,
        out_shape=(
            jax.ShapeDtypeStruct((rows, wide), F32),
            jax.ShapeDtypeStruct((rows, both - wide), F32),
        ),
        grid=(8,),
        in_specs=[pl.BlockSpec((rows // 8, both), lambda i: (i, 0))],
        out_specs=(
            pl.BlockSpec((rows // 8, wide), lambda i: (i, 0)),
            pl.BlockSpec((rows // 8, both - wide), lambda i: (i, 0)),
        ),
        compiler_params=params(58),
        name="finish",
    )(summed)


def gather_rows(ids, table, owners, capacity):
    rows, width = table.shape
    parts = width // 128
    return pl.pallas_call(
        gather_kernel,
        out_shape=jax.ShapeDtypeStruct((owners * capacity, width), BF),
        grid_spec=pltpu.PrefetchScalarGridSpec(
            num_scalar_prefetch=1,
            grid=(owners,),
            in_specs=[pl.BlockSpec((rows, width), lambda i, ids: (0, 0))],
            out_specs=pl.BlockSpec((capacity, width), lambda i, ids: (i, 0)),
            scratch_shapes=[
                pltpu.VMEM(((rows + 2) * parts, 128), F32),
                pltpu.VMEM((capacity * parts, 128), F32),
            ],
        ),
        compiler_params=params(58),
        name="gather_rows",
    )(ids, table)


def scatter_rows(ids, counts, grads, rows, owners, capacity):
    width = grads.shape[1]
    parts = 1 if width == 128 else 4
    return pl.pallas_call(
        scatter_kernel,
        out_shape=jax.ShapeDtypeStruct((width, rows), BF),
        grid_spec=pltpu.PrefetchScalarGridSpec(
            num_scalar_prefetch=2,
            grid=(owners,),
            in_specs=[pl.BlockSpec((capacity, width), lambda i, *_: (i, 0))],
            out_specs=pl.BlockSpec((width, rows), lambda i, *_: (0, 0)),
            scratch_shapes=[
                pltpu.VMEM(((rows + 8) * parts, 128), F32),
                pltpu.VMEM((capacity * parts, 128), F32),
            ],
        ),
        compiler_params=params(58),
        name="scatter_rows",
    )(ids, counts, grads)


def layer(place, arrived, slots, w_in, w_out, doc, og):
    events, width = og.shape
    wide = w_in.shape[1]
    first = (arrived.shape[0], width * 3 // 4)
    second = (arrived.shape[0], width // 4)
    vmem = pl.BlockSpec(memory_space=pltpu.VMEM)
    return pl.pallas_call(
        layer_kernel,
        in_specs=[pl.BlockSpec(memory_space=pltpu.SMEM)] + [vmem] * 6,
        out_shape=(
            jax.ShapeDtypeStruct((events, width), BF),
            jax.ShapeDtypeStruct(first, BF),
            jax.ShapeDtypeStruct(second, BF),
            jax.ShapeDtypeStruct((events, width), BF),
            jax.ShapeDtypeStruct((events, wide), BF),
            jax.ShapeDtypeStruct((events, width), BF),
        ),
        scratch_shapes=[
            pltpu.VMEM((events, width), BF),
            pltpu.VMEM((events, wide), BF),
            pltpu.VMEM((HEADS, events, events), BF),
            pltpu.VMEM((HEADS, events, events), BF),
            pltpu.VMEM((events, width), F32),
            pltpu.VMEM((events, width), BF),
            pltpu.VMEM((events, width), BF),
            pltpu.VMEM((events, 128), jnp.int32),
        ],
        compiler_params=params(60),
        name="layer",
    )(place, arrived, slots, w_in, w_out, doc, og)


def weight_grads(place, normed, du, gated, og):
    width = gated.shape[1]
    vmem = pl.BlockSpec(memory_space=pltpu.VMEM)
    return pl.pallas_call(
        weights_kernel,
        in_specs=[pl.BlockSpec(memory_space=pltpu.SMEM)] + [vmem] * 4,
        out_shape=jax.ShapeDtypeStruct((width, du.shape[1] + width), BF),
        compiler_params=params(58),
        name="weight_grads",
    )(place, normed, du, gated, og)


def other_core(value):
    return lax.ppermute(value, "dp", [(d, d ^ 1) for d in range(8)])


def along_z(value, hop):
    return lax.ppermute(value, "dp", [(d, ((d // 2 + hop) % 4) * 2 + d % 2) for d in range(8)])


def ring_sum(pieces, move):
    half = pieces.shape[1] // 2
    far = pieces[2]
    ahead = move(far[:half], 1)
    behind = move(far[half:], -1)
    up = pieces[1].astype(F32)
    up = jnp.concatenate([up[:half] + ahead.astype(F32), up[half:]], axis=0).astype(BF)
    down = pieces[3].astype(F32)
    down = jnp.concatenate([down[:half], down[half:] + behind.astype(F32)], axis=0).astype(BF)
    return pieces[0].astype(F32) + move(up, 1).astype(F32) + move(down, -1).astype(F32)


def direct_sum(pieces, move):
    total = pieces[0].astype(F32)
    for hop in range(1, 4):
        total = total + move(pieces[hop], hop).astype(F32)
    return total


def reduce_dp(value, along=ring_sum):
    both = value.reshape((2, value.shape[0] // 2) + value.shape[1:])
    mine = (both[0].astype(F32) + other_core(both[1]).astype(F32)).astype(BF)
    return along(mine.reshape((4, mine.shape[0] // 4) + mine.shape[1:]), along_z)


def whole(table, w_in, w_out, owner, local_row, doc_ids, out_grad):
    events, lookups_each = owner.shape
    rows_owned, width = table.shape
    owners = lax.axis_size("table")
    lookups = events * lookups_each
    capacity = 2 * lookups // owners
    wide = w_in.shape[1]
    own = owner.T.reshape(lookups // 128, 128)
    loc = local_row.T.reshape(lookups // 128, 128)
    slots, requests = route(own, loc, capacity, owners, rows_owned)
    asked = lax.all_to_all(requests, "table", split_axis=0, concat_axis=0, tiled=True)
    ids = asked.reshape(owners * capacity)
    counts = jnp.sum((asked < rows_owned).astype(jnp.int32), axis=1)
    found = gather_rows(ids, table, owners, capacity)
    found = found.reshape(owners, capacity, width)
    arrived = lax.all_to_all(found, "table", split_axis=0, concat_axis=0, tiled=True)
    place = lax.axis_index("dp").astype(jnp.int32).reshape(1)
    layer_out, send_a, send_b, normed, du, gated = layer(
        place, arrived.reshape(owners * capacity, width), slots, w_in, w_out, doc_ids, out_grad
    )

    def exchange(value):
        return lax.all_to_all(value, "table", split_axis=0, concat_axis=0, tiled=True)

    def scatter(value):
        return scatter_rows(
            ids, counts, value.reshape(owners * capacity, -1), rows_owned, owners, capacity
        )

    both = wide + width
    got_a = exchange(send_a.reshape(owners, capacity, -1))
    terms = weight_grads(place, normed, du, gated, out_grad)
    partial = reduce_dp(terms).astype(BF)
    lanes = width // 4
    parts = partial.reshape(owners, -1, lanes)
    got_b = exchange(
        jnp.concatenate([send_b.reshape(owners, capacity, lanes), parts], axis=1)
    )
    sum_a = scatter(got_a)
    mine = jnp.sum(got_b[:, capacity:].astype(F32), axis=0, keepdims=True).astype(BF)
    known = exchange(jnp.broadcast_to(mine, parts.shape))
    sum_b = scatter(got_b[:, :capacity])
    known = known.reshape(width // 8, both)
    gathered = lax.all_gather(known, "dp", axis=0, tiled=True)
    grad_in, grad_out = finish(gathered, wide)
    mine_a = reduce_dp(sum_a)
    mine_b = reduce_dp(sum_b, direct_sum)
    mine = jnp.concatenate([mine_a, mine_b], axis=0)
    return (layer_out, grad_in, grad_out, mine.T)


def solution(mesh):
    placed = (
        P("table", None),
        P(),
        P(),
        P(("dp", "table"), None),
        P(("dp", "table"), None),
        P(("dp", "table"), None),
        P(("dp", "table"), None),
    )
    return jax.shard_map(
        whole,
        mesh=mesh,
        in_specs=placed,
        out_specs=(P(("dp", "table"), None), P(), P(), P("table", "dp")),
        check_vma=False,
    )
```

```python
import jax
import jax.numpy as jnp
from jax import lax
from jax.experimental import pallas as pl
from jax.experimental.pallas import tpu as pltpu
from jax.sharding import PartitionSpec as P


HEADS = 4
MAXLEN = 768
EPS = 1e-06
BF = jnp.bfloat16
F32 = jnp.float32
NN = (((1,), (0,)), ((), ()))
NT = (((1,), (1,)), ((), ()))
TN = (((0,), (0,)), ((), ()))


def dot(a, b, dims=NN):
    return lax.dot_general(a, b, dims, preferred_element_type=F32)


def iota(shape, dim):
    return lax.broadcasted_iota(jnp.int32, shape, dim)


def onehot(cond):
    return jnp.where(cond, 1.0, 0.0).astype(BF)


def route_kernel(own_ref, loc_ref, slot_ref, req_ref, *, owners, capacity, dummy):
    lanes = 128
    rows = slot_ref.shape[0]

    def stacked(ref):
        many, events = ref.shape
        return jnp.concatenate(
            [
                ref[j : j + 1, k : k + lanes]
                for j in range(many)
                for k in range(0, events, lanes)
            ],
            axis=0,
        )

    own = stacked(own_ref)
    loc = stacked(loc_ref)
    member = jnp.concatenate([onehot(own == o) for o in range(owners)], axis=0)
    total = owners * rows
    upper = onehot(iota((lanes, lanes), 0) <= iota((lanes, lanes), 1))
    inside = dot(member, upper)
    left = iota((total, total), 0)
    right = iota((total, total), 1)
    before = onehot((left // rows == right // rows) & (right < left))
    offset = jnp.sum(dot(before, member), axis=1, keepdims=True)
    place = (inside + offset - 1.0) * member.astype(F32)
    position = place[0:rows]
    for o in range(1, owners):
        position = position + place[o * rows : (o + 1) * rows]
    position = position.astype(jnp.int32)
    slot_ref[...] = own * capacity + position
    who = iota((owners, lanes), 0)
    where = iota((capacity, lanes), 0)
    found = jnp.zeros((3 * owners, capacity), F32)
    for r in range(rows):
        mine = own[r : r + 1, :] == who
        row = loc[r : r + 1, :]
        high = jnp.where(mine, (row >> 8).astype(F32), 0.0).astype(BF)
        low = jnp.where(mine, (row & 255).astype(F32), 0.0).astype(BF)
        left_side = jnp.concatenate([high, low, onehot(mine)], axis=0)
        found = found + dot(left_side, onehot(position[r : r + 1, :] == where), NT)
    high = found[0:owners].astype(jnp.int32)
    low = found[owners : 2 * owners].astype(jnp.int32)
    used = found[2 * owners :] > 0.5
    req_ref[...] = jnp.where(used, high * 256 + low, dummy)


def gather_kernel(ids_ref, table_ref, out_ref, wide, picked):
    step = pl.program_id(0)
    count, width = out_ref.shape
    rows = table_ref.shape[0]
    parts = width // 128
    chunk = 64

    @pl.when(step == 0)
    def _():
        def widen(i, carry):
            base = pl.multiple_of(i * chunk, chunk)
            for c in range(parts):
                wide[pl.ds(base * parts + c, chunk, stride=parts), :] = table_ref[
                    pl.ds(base, chunk), c * 128 : (c + 1) * 128
                ].astype(F32)
            return carry

        lax.fori_loop(0, rows // chunk, widen, 0)
        wide[rows * parts : rows * parts + 8, :] = jnp.zeros((8, 128), F32)

    def copy_rows(k, carry):
        for u in range(16):
            s = k * 16 + u
            row = ids_ref[step * count + s]
            picked[pl.ds(pl.multiple_of(s * parts, parts), parts), :] = wide[
                pl.ds(pl.multiple_of(row * parts, parts), parts), :
            ]
        return carry

    lax.fori_loop(0, count // 16, copy_rows, 0)
    for c in range(parts):
        out_ref[:, c * 128 : (c + 1) * 128] = picked[pl.ds(c, count, stride=parts), :].astype(BF)


def scatter_kernel(ids_ref, cnt_ref, grad_ref, keep_ref, give_ref, total, rows_in):
    step = pl.program_id(0)
    count, width = grad_ref.shape
    used = width // 128
    half, rows = keep_ref.shape
    parts = rows_in.shape[0] // count

    @pl.when(step == 0)
    def _():
        def clear(i, carry):
            total[pl.ds(pl.multiple_of(i * 256, 256), 256), :] = jnp.zeros((256, 128), F32)
            return carry

        lax.fori_loop(0, rows * parts // 256, clear, 0)

    for c in range(used):
        rows_in[pl.ds(c, count, stride=parts), :] = grad_ref[:, c * 128 : (c + 1) * 128].astype(F32)

    def add_rows(k, carry):
        for u in range(8):
            s = k * 8 + u
            row = ids_ref[step * count + s]
            at = pl.ds(pl.multiple_of(row * parts, parts), parts)
            total[at, :] = (
                total[at, :] + rows_in[pl.ds(pl.multiple_of(s * parts, parts), parts), :]
            )
        return carry

    lax.fori_loop(0, (cnt_ref[step] + 7) // 8, add_rows, 0)

    @pl.when(step == pl.num_programs(0) - 1)
    def _():
        def flush(i, carry):
            for c in range(used):
                block = total[pl.ds(i * (128 * parts) + c, 128, stride=parts), :].T.astype(BF)
                at = pl.ds(pl.multiple_of(i * 128, 128), 128)
                for q in range(2):
                    start = c * 128 + q * 64
                    out_ref = keep_ref if start < half else give_ref
                    out_ref[start % half : start % half + 64, at] = block[q * 64 : (q + 1) * 64]
            return carry

        lax.fori_loop(0, rows // 128, flush, 0)


def normal(values):
    center = values - jnp.mean(values, axis=-1, keepdims=True)
    spread = jnp.mean(center * center, axis=-1, keepdims=True)
    scale = lax.rsqrt(spread + EPS)
    return center * scale, scale


def normal_back(grad, unit, scale):
    shared = jnp.mean(grad, axis=-1, keepdims=True)
    along = jnp.mean(grad * unit, axis=-1, keepdims=True)
    return scale * (grad - shared - unit * along)


def spread_columns(place_ref, width, shares):
    column = iota((8, width), 1)
    place = place_ref[0]
    source = jnp.zeros((8, width), jnp.int32)
    start = 0
    for share in shares:
        inside = column - 8 * start
        piece = inside // share
        z = (place // 2 + piece) & 3
        core = (place + piece // 4) & 1
        here = (z * 2 + core) * (width // 8) + start + inside - piece * share
        source = jnp.where(inside >= 0, here, source)
        start += share
    return onehot(iota((width, width), 0) == source[0:1, :])


def layer_kernel(
    place_ref,
    arrived_ref,
    slot_ref,
    w_in_ref,
    w_out_ref,
    doc_ref,
    og_ref,
    out_ref,
    send_a_ref,
    send_b_ref,
    normed_ref,
    du_ref,
    gated_ref,
    emb_ref,
    proj_ref,
    wts_ref,
    dws_ref,
    mixed_ref,
    dmix_ref,
    eg_ref,
    col_ref,
):
    events, width = og_ref.shape
    slots = arrived_ref.shape[0]
    head = width // HEADS
    blk = 256
    nblk = events // blk
    lane_rows = events // 128
    cap_step = 256
    slot_all = slot_ref[...]
    slot_cols = slot_all.astype(F32).T.astype(jnp.int32)
    doc_rows = doc_ref[...]
    for r in range(lane_rows):
        rows = slice(r * 128, (r + 1) * 128)
        col_ref[rows, 0:1] = slot_cols[:, r : r + 1]
        col_ref[rows, 1:2] = slot_cols[:, lane_rows + r : lane_rows + r + 1]
    doc_cols = jnp.broadcast_to(doc_rows.astype(F32), (8, events)).T[:, 0:1].astype(jnp.int32)
    col_ref[:, 2:3] = doc_cols
    scale = head ** (-0.5)

    def steps(body, total, group):
        def several(k, carry):
            for u in range(group):
                body(k * group + u, carry)
            return carry

        if total == group:
            several(0, 0)
        else:
            lax.fori_loop(0, total // group, several, 0)

    def block_rows(b):
        return pl.ds(pl.multiple_of(b * blk, blk), blk)

    def unpack(b, carry):
        rows = block_rows(b)
        first = col_ref[rows, 0:1]
        second = col_ref[rows, 1:2]
        total = jnp.zeros((blk, width), F32)
        for o in range(slots // cap_step):
            where = iota((blk, cap_step), 1) + o * cap_step
            pick = onehot((where == first) | (where == second))
            total = total + dot(pick, arrived_ref[o * cap_step : (o + 1) * cap_step, :])
        embedded = total.astype(BF)
        emb_ref[rows, :] = embedded
        unit, _ = normal(embedded.astype(F32))
        normed = unit.astype(BF)
        normed_ref[rows, :] = normed
        for c in range(4):
            cols = slice(c * width, (c + 1) * width)
            u = dot(normed, w_in_ref[:, cols])
            sig = 0.5 * jnp.tanh(0.5 * u) + 0.5
            act = u * sig
            proj_ref[rows, cols] = act.astype(BF)
            du_ref[rows, cols] = (sig + act * (1.0 - sig)).astype(BF)
        return carry

    steps(unpack, nblk, 2)

    def heads_forward(h, carry):
        def cols(part):
            return pl.ds(pl.multiple_of(part * width + h * head, head), head)

        mine = pl.ds(pl.multiple_of(h * head, head), head)
        for i in range(nblk):
            rows = slice(i * blk, (i + 1) * blk)
            query = proj_ref[rows, cols(2)]
            total = jnp.zeros((blk, head), F32)
            for j in range(i + 1):
                keys = slice(j * blk, (j + 1) * blk)
                scores = dot(query, proj_ref[keys, cols(3)], NT) * scale
                allowed = col_ref[rows, 2:3] == doc_rows[:, keys]
                if i == j:
                    allowed = allowed & (iota((blk, blk), 0) >= iota((blk, blk), 1))
                sig = 0.5 * jnp.tanh(0.5 * scores) + 0.5
                act = scores * sig
                weight = jnp.where(allowed, act * (1.0 / MAXLEN), 0.0).astype(BF)
                slope = sig + act * (1.0 - sig)
                wts_ref[h, rows, keys] = weight
                dws_ref[h, rows, keys] = jnp.where(allowed, slope * (scale / MAXLEN), 0.0).astype(BF)
                total = total + dot(weight, proj_ref[keys, cols(1)])
            mixed_ref[rows, mine] = total
        return carry

    lax.fori_loop(0, HEADS, heads_forward, 0)

    def middle(b, carry):
        rows = block_rows(b)
        unit, spread = normal(mixed_ref[rows, :])
        gate = proj_ref[rows, 0:width].astype(F32)
        gated = (unit * gate).astype(BF)
        gated_ref[rows, :] = gated
        out_ref[rows, :] = (emb_ref[rows, :].astype(F32) + dot(gated, w_out_ref[...])).astype(BF)
        dgated = dot(og_ref[rows, :], w_out_ref[...], NT).astype(BF).astype(F32)
        dmix_ref[rows, :] = normal_back(dgated * gate, unit, spread).astype(BF)
        dgate = (dgated * unit).astype(BF).astype(F32)
        du_ref[rows, 0:width] = (dgate * du_ref[rows, 0:width].astype(F32)).astype(BF)
        return carry

    steps(middle, nblk, 1)

    def heads_backward(h, carry):
        def cols(part):
            return pl.ds(pl.multiple_of(part * width + h * head, head), head)

        mine = pl.ds(pl.multiple_of(h * head, head), head)

        def put(rows, part, value):
            at = cols(part)
            du_ref[rows, at] = (
                value.astype(BF).astype(F32) * du_ref[rows, at].astype(F32)
            ).astype(BF)

        for j in range(nblk):
            keys = slice(j * blk, (j + 1) * blk)
            value = proj_ref[keys, cols(1)]
            dkey = jnp.zeros((blk, head), F32)
            dvalue = jnp.zeros((blk, head), F32)
            for i in range(j, nblk):
                rows = slice(i * blk, (i + 1) * blk)
                dmix = dmix_ref[rows, mine]
                dscore = (
                    dot(dmix, value, NT) * dws_ref[h, rows, keys].astype(F32)
                ).astype(BF)
                dws_ref[h, rows, keys] = dscore
                dvalue = dvalue + dot(wts_ref[h, rows, keys], dmix, TN)
                dkey = dkey + dot(dscore, proj_ref[rows, cols(2)], TN)
            put(keys, 1, dvalue)
            put(keys, 3, dkey)
        for i in range(nblk):
            rows = slice(i * blk, (i + 1) * blk)
            upto = slice(0, (i + 1) * blk)
            put(rows, 2, dot(dws_ref[h, rows, upto], proj_ref[upto, cols(3)]))
        return carry

    lax.fori_loop(0, HEADS, heads_backward, 0)

    spread = spread_columns(place_ref, width, (send_a_ref.shape[1] // 8, send_b_ref.shape[1] // 8))

    def last(b, carry):
        rows = block_rows(b)
        dnormed = dot(du_ref[rows, :], w_in_ref[...], NT).astype(BF).astype(F32)
        unit, size = normal(emb_ref[rows, :].astype(F32))
        grad = normal_back(dnormed, unit, size) + og_ref[rows, :].astype(F32)
        eg_ref[rows, :] = dot(grad.astype(BF), spread).astype(BF)
        return carry

    steps(last, nblk, 1)

    def pack(o, carry):
        where = iota((cap_step, 128), 0) + o * cap_step
        picks = [
            onehot(
                (where == slot_all[r : r + 1, :])
                | (where == slot_all[lane_rows + r : lane_rows + r + 1, :])
            )
            for r in range(lane_rows)
        ]
        packed = dot(jnp.concatenate(picks, axis=1), eg_ref[...]).astype(BF)
        at = pl.ds(pl.multiple_of(o * cap_step, cap_step), cap_step)
        send_a_ref[at, :] = packed[:, : send_a_ref.shape[1]]
        send_b_ref[at, :] = packed[:, send_a_ref.shape[1] :]
        return carry

    steps(pack, slots // cap_step, 16)


def weights_kernel(place_ref, normed_ref, du_ref, gated_ref, og_ref, keep_ref, give_ref, turned):
    step = pl.program_id(0)
    last = pl.num_programs(0) - 1
    width = gated_ref.shape[1]
    half = width // 2

    @pl.when(step == 0)
    def _():
        spread = spread_columns(place_ref, width, (width // 8,))
        turned[0] = dot(normed_ref[...], spread).astype(BF)
        turned[1] = dot(gated_ref[...], spread).astype(BF)

    def put(value):
        keep_ref[...] = value[:half].astype(BF)
        give_ref[...] = value[half:].astype(BF)

    @pl.when(step < last)
    def _():
        put(dot(turned[0], du_ref[...], TN))

    @pl.when(step == last)
    def _():
        put(dot(turned[1], og_ref[...], TN))


def finish_kernel(sum_ref, first_ref, second_ref):
    wide = first_ref.shape[1]
    first_ref[...] = sum_ref[:, :wide].astype(F32)
    second_ref[...] = sum_ref[:, wide:].astype(F32)


def params(mib, **more):
    return pltpu.CompilerParams(vmem_limit_bytes=mib * 2**20, **more)


def route(own, loc, capacity, owners, dummy):
    return pl.pallas_call(
        lambda *refs: route_kernel(*refs, owners=owners, capacity=capacity, dummy=dummy),
        out_shape=(
            jax.ShapeDtypeStruct((own.size // 128, 128), jnp.int32),
            jax.ShapeDtypeStruct((owners, capacity), jnp.int32),
        ),
        name="route",
    )(own, loc)


def finish(summed, wide):
    rows, both = summed.shape
    return pl.pallas_call(
        finish_kernel,
        out_shape=(
            jax.ShapeDtypeStruct((rows, wide), F32),
            jax.ShapeDtypeStruct((rows, both - wide), F32),
        ),
        grid=(8,),
        in_specs=[pl.BlockSpec((rows // 8, both), lambda i: (i, 0))],
        out_specs=(
            pl.BlockSpec((rows // 8, wide), lambda i: (i, 0)),
            pl.BlockSpec((rows // 8, both - wide), lambda i: (i, 0)),
        ),
        compiler_params=params(16),
        name="finish",
    )(summed)


def gather_rows(ids, table, owners, capacity):
    rows, width = table.shape
    parts = width // 128
    return pl.pallas_call(
        gather_kernel,
        out_shape=jax.ShapeDtypeStruct((owners * capacity, width), BF),
        grid_spec=pltpu.PrefetchScalarGridSpec(
            num_scalar_prefetch=1,
            grid=(owners,),
            in_specs=[pl.BlockSpec((rows, width), lambda i, ids: (0, 0))],
            out_specs=pl.BlockSpec((capacity, width), lambda i, ids: (i, 0)),
            scratch_shapes=[
                pltpu.VMEM(((rows + 2) * parts, 128), F32),
                pltpu.VMEM((capacity * parts, 128), F32),
            ],
        ),
        compiler_params=params(32),
        name="gather_rows",
    )(ids, table)


def scatter_rows(ids, counts, grads, rows, owners, capacity):
    width = grads.shape[2]
    parts = 1 if width == 128 else 4
    return pl.pallas_call(
        scatter_kernel,
        out_shape=(jax.ShapeDtypeStruct((width // 2, rows), BF),) * 2,
        grid_spec=pltpu.PrefetchScalarGridSpec(
            num_scalar_prefetch=2,
            grid=(owners,),
            in_specs=[pl.BlockSpec((None, capacity, width), lambda i, *_: (i, 0, 0))],
            out_specs=(pl.BlockSpec((width // 2, rows), lambda i, *_: (0, 0)),) * 2,
            scratch_shapes=[
                pltpu.VMEM(((rows + 8) * parts, 128), F32),
                pltpu.VMEM((capacity * parts, 128), F32),
            ],
        ),
        compiler_params=params(40),
        name="scatter_rows",
    )(ids, counts, grads)


def layer(place, arrived, slots, w_in, w_out, doc, og):
    events, width = og.shape
    wide = w_in.shape[1]
    first = (arrived.shape[0], width * 3 // 4)
    second = (arrived.shape[0], width // 4)
    vmem = pl.BlockSpec(memory_space=pltpu.VMEM)
    return pl.pallas_call(
        layer_kernel,
        in_specs=[pl.BlockSpec(memory_space=pltpu.SMEM)] + [vmem] * 6,
        out_shape=(
            jax.ShapeDtypeStruct((events, width), BF),
            jax.ShapeDtypeStruct(first, BF),
            jax.ShapeDtypeStruct(second, BF),
            jax.ShapeDtypeStruct((events, width), BF),
            jax.ShapeDtypeStruct((events, wide), BF),
            jax.ShapeDtypeStruct((events, width), BF),
        ),
        scratch_shapes=[
            pltpu.VMEM((events, width), BF),
            pltpu.VMEM((events, wide), BF),
            pltpu.VMEM((HEADS, events, events), BF),
            pltpu.VMEM((HEADS, events, events), BF),
            pltpu.VMEM((events, width), F32),
            pltpu.VMEM((events, width), BF),
            pltpu.VMEM((events, width), BF),
            pltpu.VMEM((events, 128), jnp.int32),
        ],
        compiler_params=params(60),
        name="layer",
    )(place, arrived, slots, w_in, w_out, doc, og)


def weight_grads(place, normed, du, gated, og):
    events, width = gated.shape
    steps = du.shape[1] // width
    whole = pl.BlockSpec((events, width), lambda c: (0, 0))
    part = pl.BlockSpec((width // 2, width), lambda c: (0, c))
    return pl.pallas_call(
        weights_kernel,
        grid=(steps + 1,),
        in_specs=[
            pl.BlockSpec(memory_space=pltpu.SMEM),
            whole,
            pl.BlockSpec((events, width), lambda c: (0, jnp.minimum(c, steps - 1))),
            whole,
            whole,
        ],
        out_specs=(part, part),
        out_shape=(jax.ShapeDtypeStruct((width // 2, du.shape[1] + width), BF),) * 2,
        scratch_shapes=[pltpu.VMEM((2, events, width), BF)],
        compiler_params=params(58),
        name="weight_grads",
    )(place, normed, du, gated, og)


def other_core(value):
    return lax.ppermute(value, "dp", [(d, d ^ 1) for d in range(8)])


def along_z(value, hop):
    return lax.ppermute(value, "dp", [(d, ((d // 2 + hop) % 4) * 2 + d % 2) for d in range(8)])


def ring_sum(pieces, move):
    half = pieces.shape[1] // 2
    far = pieces[2]
    ahead = move(far[:half], 1)
    behind = move(far[half:], -1)
    up = pieces[1].astype(F32)
    up = jnp.concatenate([up[:half] + ahead.astype(F32), up[half:]], axis=0).astype(BF)
    down = pieces[3].astype(F32)
    down = jnp.concatenate([down[:half], down[half:] + behind.astype(F32)], axis=0).astype(BF)
    return pieces[0].astype(F32) + move(up, 1).astype(F32) + move(down, -1).astype(F32)


def direct_sum(pieces, move):
    total = pieces[0].astype(F32)
    moved = [move(pieces[hop], hop) for hop in range(1, 4)]
    for value in moved:
        total = total + value.astype(F32)
    return total


def reduce_dp(value, along=ring_sum):
    keep, give = value
    mine = (keep.astype(F32) + other_core(give).astype(F32)).astype(BF)
    return along(mine.reshape((4, mine.shape[0] // 4) + mine.shape[1:]), along_z)


def whole(table, w_in, w_out, owner, local_row, doc_ids, out_grad):
    events, lookups_each = owner.shape
    rows_owned, width = table.shape
    owners = lax.axis_size("table")
    lookups = events * lookups_each
    capacity = 2 * lookups // owners
    wide = w_in.shape[1]
    slots, requests = route(owner.T, local_row.T, capacity, owners, rows_owned)
    asked = lax.all_to_all(requests, "table", split_axis=0, concat_axis=0, tiled=True)
    ids = asked.reshape(owners * capacity)
    counts = jnp.sum((asked < rows_owned).astype(jnp.int32), axis=1)
    found = gather_rows(ids, table, owners, capacity)
    found = found.reshape(owners, capacity, width)
    arrived = lax.all_to_all(found, "table", split_axis=0, concat_axis=0, tiled=True)
    place = lax.axis_index("dp").astype(jnp.int32).reshape(1)
    layer_out, send_a, send_b, normed, du, gated = layer(
        place, arrived.reshape(owners * capacity, width), slots, w_in, w_out, doc_ids, out_grad
    )

    def exchange(value):
        return lax.all_to_all(value, "table", split_axis=0, concat_axis=0, tiled=True)

    def scatter(value):
        return scatter_rows(ids, counts, value, rows_owned, owners, capacity)

    both = wide + width
    got_a = exchange(send_a.reshape(owners, capacity, -1))
    terms = weight_grads(place, normed, du, gated, out_grad)
    partial = reduce_dp(terms).astype(BF)
    lanes = width // 4
    parts = partial.reshape(owners, -1, lanes)
    got_b = exchange(
        jnp.concatenate([send_b.reshape(owners, capacity, lanes), parts], axis=1)
    )
    sum_a = scatter(got_a)
    mine = jnp.sum(got_b[:, capacity:].astype(F32), axis=0, keepdims=True).astype(BF)
    known = exchange(jnp.broadcast_to(mine, parts.shape))
    sum_b = scatter(got_b)
    known = known.reshape(width // 8, both)
    gathered = lax.all_gather(known, "dp", axis=0, tiled=True)
    grad_in, grad_out = finish(gathered, wide)
    mine_a = reduce_dp(sum_a)
    mine_b = reduce_dp(sum_b, direct_sum)
    mine = jnp.concatenate([mine_a, mine_b], axis=0)
    return (layer_out, grad_in, grad_out, mine.T)


def solution(mesh):
    placed = (
        P("table", None),
        P(),
        P(),
        P(("dp", "table"), None),
        P(("dp", "table"), None),
        P(("dp", "table"), None),
        P(("dp", "table"), None),
    )
    return jax.shard_map(
        whole,
        mesh=mesh,
        in_specs=placed,
        out_specs=(P(("dp", "table"), None), P(), P(), P("table", "dp")),
        check_vma=False,
    )
```

```python
import jax
import jax.numpy as jnp
from jax import lax
from jax.experimental import pallas as pl
from jax.experimental.pallas import tpu as pltpu
from jax.sharding import PartitionSpec as P


HEADS = 4
MAXLEN = 768
EPS = 1e-06
GROUP = 16
STEPS = 4
BF = jnp.bfloat16
F32 = jnp.float32
NN = (((1,), (0,)), ((), ()))
NT = (((1,), (1,)), ((), ()))
TN = (((0,), (0,)), ((), ()))


def dot(a, b, dims=NN):
    return lax.dot_general(a, b, dims, preferred_element_type=F32)


def iota(shape, dim):
    return lax.broadcasted_iota(jnp.int32, shape, dim)


def onehot(cond):
    return jnp.where(cond, 1.0, 0.0).astype(BF)


def route_kernel(own_ref, loc_ref, slot_ref, req_ref, *, owners, capacity, dummy, width):
    lanes = 128
    rows = slot_ref.shape[0]

    def stacked(ref):
        many, events = ref.shape
        return jnp.concatenate(
            [
                ref[j : j + 1, k : k + lanes]
                for j in range(many)
                for k in range(0, events, lanes)
            ],
            axis=0,
        )

    own = stacked(own_ref)
    loc = stacked(loc_ref)
    member = jnp.concatenate([onehot(own == o) for o in range(owners)], axis=0)
    total = owners * rows
    upper = onehot(iota((lanes, lanes), 0) <= iota((lanes, lanes), 1))
    inside = dot(member, upper)
    left = iota((total, total), 0)
    right = iota((total, total), 1)
    before = onehot((left // rows == right // rows) & (right < left))
    offset = jnp.sum(dot(before, member), axis=1, keepdims=True)
    place = (inside + offset - 1.0) * member.astype(F32)
    position = place[0:rows]
    for o in range(1, owners):
        position = position + place[o * rows : (o + 1) * rows]
    position = position.astype(jnp.int32)
    slot_ref[...] = own * capacity + position
    who = iota((owners, lanes), 0)
    where = iota((capacity, lanes), 0)
    found = jnp.zeros((3 * owners, capacity), F32)
    for r in range(rows):
        mine = own[r : r + 1, :] == who
        row = loc[r : r + 1, :]
        high = jnp.where(mine, (row >> 8).astype(F32), 0.0).astype(BF)
        low = jnp.where(mine, (row & 255).astype(F32), 0.0).astype(BF)
        left_side = jnp.concatenate([high, low, onehot(mine)], axis=0)
        found = found + dot(left_side, onehot(position[r : r + 1, :] == where), NT)
    high = found[0:owners].astype(jnp.int32)
    low = found[owners : 2 * owners].astype(jnp.int32)
    used = found[2 * owners :] > 0.5
    req_ref[...] = jnp.where(used, high * 256 + low, dummy) * (width // 128)


def gather_kernel(ids_ref, table_ref, out_ref, wide, picked):
    step = pl.program_id(0)
    count, width = out_ref.shape
    rows = table_ref.shape[0]
    parts = width // 128
    chunk = 64

    @pl.when(step == 0)
    def _():
        def widen(i, carry):
            base = pl.multiple_of(i * chunk, chunk)
            for c in range(parts):
                wide[pl.ds(base * parts + c, chunk, stride=parts), :] = table_ref[
                    pl.ds(base, chunk), c * 128 : (c + 1) * 128
                ].astype(F32)
            return carry

        lax.fori_loop(0, rows // chunk, widen, 0)
        wide[rows * parts : rows * parts + 8, :] = jnp.zeros((8, 128), F32)

    def copy_rows(k, carry):
        base = step * count + k * 16
        taken = k * (16 * parts)
        for u in range(16):
            row = ids_ref[base + u]
            picked[pl.ds(pl.multiple_of(taken + u * parts, parts), parts), :] = wide[
                pl.ds(pl.multiple_of(row, parts), parts), :
            ]
        return carry

    lax.fori_loop(0, count // 16, copy_rows, 0)
    for c in range(parts):
        out_ref[:, c * 128 : (c + 1) * 128] = picked[pl.ds(c, count, stride=parts), :].astype(BF)


def scatter_kernel(ids_ref, cnt_ref, grad_ref, keep_ref, give_ref, total, rows_in):
    step = pl.program_id(0)
    sources, count, width = grad_ref.shape
    used = width // 128
    half, rows = keep_ref.shape
    parts = rows_in.shape[0] // (sources * count)

    @pl.when(step == 0)
    def _():
        def clear(i, carry):
            total[pl.ds(pl.multiple_of(i * 256, 256), 256), :] = jnp.zeros((256, 128), F32)
            return carry

        lax.fori_loop(0, rows * parts // 256, clear, 0)

    for q in range(sources):
        for c in range(used):
            rows_in[pl.ds(q * count * parts + c, count, stride=parts), :] = grad_ref[
                q, :, c * 128 : (c + 1) * 128
            ].astype(F32)

    def add_rows(q, k):
        base = (step * sources + q) * count + k * GROUP
        taken = (q * count + k * GROUP) * parts
        for u in range(0, GROUP, 2):
            one = ids_ref[base + u]
            two = ids_ref[base + (u + 1)]
            first = pl.ds(pl.multiple_of(one, parts), parts)
            second = pl.ds(pl.multiple_of(two, parts), parts)
            left = rows_in[pl.ds(pl.multiple_of(taken + u * parts, parts), parts), :]
            right = rows_in[pl.ds(pl.multiple_of(taken + (u + 1) * parts, parts), parts), :]
            both = jnp.where(one == two, 1.0, 0.0)
            sum_one = total[first, :] + left
            sum_two = total[second, :] + (right + left * both)
            total[first, :] = sum_one
            total[second, :] = sum_two

    def add_source(q, carry):
        def group(k, inner):
            add_rows(q, k)
            return inner

        lax.fori_loop(0, (cnt_ref[step * sources + q] + (GROUP - 1)) // GROUP, group, 0)
        return carry

    lax.fori_loop(0, sources, add_source, 0)

    @pl.when(step == pl.num_programs(0) - 1)
    def _():
        def flush(i, carry):
            for c in range(used):
                block = total[pl.ds(i * (128 * parts) + c, 128, stride=parts), :].T.astype(BF)
                at = pl.ds(pl.multiple_of(i * 128, 128), 128)
                for q in range(2):
                    start = c * 128 + q * 64
                    out_ref = keep_ref if start < half else give_ref
                    out_ref[start % half : start % half + 64, at] = block[q * 64 : (q + 1) * 64]
            return carry

        lax.fori_loop(0, rows // 128, flush, 0)


def normal(values):
    center = values - jnp.mean(values, axis=-1, keepdims=True)
    spread = jnp.mean(center * center, axis=-1, keepdims=True)
    scale = lax.rsqrt(spread + EPS)
    return center * scale, scale


def normal_back(grad, unit, scale):
    shared = jnp.mean(grad, axis=-1, keepdims=True)
    along = jnp.mean(grad * unit, axis=-1, keepdims=True)
    return scale * (grad - shared - unit * along)


def spread_columns(place_ref, width, shares):
    column = iota((8, width), 1)
    place = place_ref[0]
    source = jnp.zeros((8, width), jnp.int32)
    start = 0
    for share in shares:
        inside = column - 8 * start
        piece = inside // share
        z = (place // 2 + piece) & 3
        core = (place + piece // 4) & 1
        here = (z * 2 + core) * (width // 8) + start + inside - piece * share
        source = jnp.where(inside >= 0, here, source)
        start += share
    return onehot(iota((width, width), 0) == source[0:1, :])


def layer_kernel(
    place_ref,
    arrived_ref,
    slot_ref,
    w_in_ref,
    w_out_ref,
    doc_ref,
    og_ref,
    out_ref,
    send_a_ref,
    send_b_ref,
    normed_ref,
    du_ref,
    gated_ref,
    emb_ref,
    proj_ref,
    wts_ref,
    dws_ref,
    mixed_ref,
    dmix_ref,
    eg_ref,
    col_ref,
):
    events, width = og_ref.shape
    slots = arrived_ref.shape[0]
    head = width // HEADS
    blk = 256
    nblk = events // blk
    lane_rows = events // 128
    cap_step = 256
    slot_all = slot_ref[...]
    slot_cols = slot_all.astype(F32).T.astype(jnp.int32)
    doc_rows = doc_ref[...]
    for r in range(lane_rows):
        rows = slice(r * 128, (r + 1) * 128)
        col_ref[rows, 0:1] = slot_cols[:, r : r + 1]
        col_ref[rows, 1:2] = slot_cols[:, lane_rows + r : lane_rows + r + 1]
    doc_cols = jnp.broadcast_to(doc_rows.astype(F32), (8, events)).T[:, 0:1].astype(jnp.int32)
    col_ref[:, 2:3] = doc_cols
    scale = head ** (-0.5)

    def steps(body, total, group):
        def several(k, carry):
            for u in range(group):
                body(k * group + u, carry)
            return carry

        if total == group:
            several(0, 0)
        else:
            lax.fori_loop(0, total // group, several, 0)

    def block_rows(b):
        return pl.ds(pl.multiple_of(b * blk, blk), blk)

    def unpack(b, carry):
        rows = block_rows(b)
        first = col_ref[rows, 0:1]
        second = col_ref[rows, 1:2]
        total = jnp.zeros((blk, width), F32)
        for o in range(slots // cap_step):
            where = iota((blk, cap_step), 1) + o * cap_step
            pick = onehot((where == first) | (where == second))
            total = total + dot(pick, arrived_ref[o * cap_step : (o + 1) * cap_step, :])
        embedded = total.astype(BF)
        emb_ref[rows, :] = embedded
        unit, _ = normal(embedded.astype(F32))
        normed = unit.astype(BF)
        normed_ref[rows, :] = normed
        for c in range(4):
            cols = slice(c * width, (c + 1) * width)
            u = dot(normed, w_in_ref[:, cols])
            sig = 0.5 * jnp.tanh(0.5 * u) + 0.5
            act = u * sig
            proj_ref[rows, cols] = act.astype(BF)
            du_ref[rows, cols] = (sig + act * (1.0 - sig)).astype(BF)
        return carry

    steps(unpack, nblk, 2)

    def heads_forward(h, carry):
        def cols(part):
            return pl.ds(pl.multiple_of(part * width + h * head, head), head)

        mine = pl.ds(pl.multiple_of(h * head, head), head)
        for i in range(nblk):
            rows = slice(i * blk, (i + 1) * blk)
            query = proj_ref[rows, cols(2)]
            total = jnp.zeros((blk, head), F32)
            for j in range(i + 1):
                keys = slice(j * blk, (j + 1) * blk)
                scores = dot(query, proj_ref[keys, cols(3)], NT) * scale
                allowed = col_ref[rows, 2:3] == doc_rows[:, keys]
                if i == j:
                    allowed = allowed & (iota((blk, blk), 0) >= iota((blk, blk), 1))
                sig = 0.5 * jnp.tanh(0.5 * scores) + 0.5
                act = scores * sig
                weight = jnp.where(allowed, act * (1.0 / MAXLEN), 0.0).astype(BF)
                slope = sig + act * (1.0 - sig)
                wts_ref[h, rows, keys] = weight
                dws_ref[h, rows, keys] = jnp.where(allowed, slope * (scale / MAXLEN), 0.0).astype(BF)
                total = total + dot(weight, proj_ref[keys, cols(1)])
            mixed_ref[rows, mine] = total
        return carry

    lax.fori_loop(0, HEADS, heads_forward, 0)

    def middle(b, carry):
        rows = block_rows(b)
        unit, spread = normal(mixed_ref[rows, :])
        gate = proj_ref[rows, 0:width].astype(F32)
        gated = (unit * gate).astype(BF)
        gated_ref[rows, :] = gated
        out_ref[rows, :] = (emb_ref[rows, :].astype(F32) + dot(gated, w_out_ref[...])).astype(BF)
        dgated = dot(og_ref[rows, :], w_out_ref[...], NT).astype(BF).astype(F32)
        dmix_ref[rows, :] = normal_back(dgated * gate, unit, spread).astype(BF)
        dgate = (dgated * unit).astype(BF).astype(F32)
        du_ref[rows, 0:width] = (dgate * du_ref[rows, 0:width].astype(F32)).astype(BF)
        return carry

    steps(middle, nblk, 1)

    def heads_backward(h, carry):
        def cols(part):
            return pl.ds(pl.multiple_of(part * width + h * head, head), head)

        mine = pl.ds(pl.multiple_of(h * head, head), head)

        def put(rows, part, value):
            at = cols(part)
            du_ref[rows, at] = (
                value.astype(BF).astype(F32) * du_ref[rows, at].astype(F32)
            ).astype(BF)

        for j in range(nblk):
            keys = slice(j * blk, (j + 1) * blk)
            value = proj_ref[keys, cols(1)]
            dkey = jnp.zeros((blk, head), F32)
            dvalue = jnp.zeros((blk, head), F32)
            for i in range(j, nblk):
                rows = slice(i * blk, (i + 1) * blk)
                dmix = dmix_ref[rows, mine]
                dscore = (
                    dot(dmix, value, NT) * dws_ref[h, rows, keys].astype(F32)
                ).astype(BF)
                dws_ref[h, rows, keys] = dscore
                dvalue = dvalue + dot(wts_ref[h, rows, keys], dmix, TN)
                dkey = dkey + dot(dscore, proj_ref[rows, cols(2)], TN)
            put(keys, 1, dvalue)
            put(keys, 3, dkey)
        for i in range(nblk):
            rows = slice(i * blk, (i + 1) * blk)
            upto = slice(0, (i + 1) * blk)
            put(rows, 2, dot(dws_ref[h, rows, upto], proj_ref[upto, cols(3)]))
        return carry

    lax.fori_loop(0, HEADS, heads_backward, 0)

    spread = spread_columns(place_ref, width, (send_a_ref.shape[1] // 8, send_b_ref.shape[1] // 8))

    def last(b, carry):
        rows = block_rows(b)
        dnormed = dot(du_ref[rows, :], w_in_ref[...], NT).astype(BF).astype(F32)
        unit, size = normal(emb_ref[rows, :].astype(F32))
        grad = normal_back(dnormed, unit, size) + og_ref[rows, :].astype(F32)
        eg_ref[rows, :] = dot(grad.astype(BF), spread).astype(BF)
        return carry

    steps(last, nblk, 1)

    def pack(o, carry):
        where = iota((cap_step, 128), 0) + o * cap_step
        picks = [
            onehot(
                (where == slot_all[r : r + 1, :])
                | (where == slot_all[lane_rows + r : lane_rows + r + 1, :])
            )
            for r in range(lane_rows)
        ]
        packed = dot(jnp.concatenate(picks, axis=1), eg_ref[...]).astype(BF)
        at = pl.ds(pl.multiple_of(o * cap_step, cap_step), cap_step)
        send_a_ref[at, :] = packed[:, : send_a_ref.shape[1]]
        send_b_ref[at, :] = packed[:, send_a_ref.shape[1] :]
        return carry

    steps(pack, slots // cap_step, 16)


def weights_kernel(place_ref, normed_ref, du_ref, gated_ref, og_ref, keep_ref, give_ref, turned):
    step = pl.program_id(0)
    last = pl.num_programs(0) - 1
    width = gated_ref.shape[1]
    half = width // 2

    @pl.when(step == 0)
    def _():
        spread = spread_columns(place_ref, width, (width // 8,))
        turned[0] = dot(normed_ref[...], spread).astype(BF)
        turned[1] = dot(gated_ref[...], spread).astype(BF)

    def put(value):
        keep_ref[...] = value[:half].astype(BF)
        give_ref[...] = value[half:].astype(BF)

    @pl.when(step < last)
    def _():
        put(dot(turned[0], du_ref[...], TN))

    @pl.when(step == last)
    def _():
        put(dot(turned[1], og_ref[...], TN))


def finish_kernel(sum_ref, first_ref, second_ref):
    wide = first_ref.shape[1]
    first_ref[...] = sum_ref[:, :wide].astype(F32)
    second_ref[...] = sum_ref[:, wide:].astype(F32)


def params(mib, **more):
    return pltpu.CompilerParams(vmem_limit_bytes=mib * 2**20, **more)


def route(own, loc, capacity, owners, dummy, width):
    return pl.pallas_call(
        lambda *refs: route_kernel(*refs, owners=owners, capacity=capacity, dummy=dummy, width=width),
        out_shape=(
            jax.ShapeDtypeStruct((own.size // 128, 128), jnp.int32),
            jax.ShapeDtypeStruct((owners, capacity), jnp.int32),
        ),
        name="route",
    )(own, loc)


def finish(summed, wide):
    rows, both = summed.shape
    return pl.pallas_call(
        finish_kernel,
        out_shape=(
            jax.ShapeDtypeStruct((rows, wide), F32),
            jax.ShapeDtypeStruct((rows, both - wide), F32),
        ),
        grid=(8,),
        in_specs=[pl.BlockSpec((rows // 8, both), lambda i: (i, 0))],
        out_specs=(
            pl.BlockSpec((rows // 8, wide), lambda i: (i, 0)),
            pl.BlockSpec((rows // 8, both - wide), lambda i: (i, 0)),
        ),
        compiler_params=params(16),
        name="finish",
    )(summed)


def gather_rows(ids, table, owners, capacity):
    rows, width = table.shape
    parts = width // 128
    block = owners * capacity // STEPS
    return pl.pallas_call(
        gather_kernel,
        out_shape=jax.ShapeDtypeStruct((owners * capacity, width), BF),
        grid_spec=pltpu.PrefetchScalarGridSpec(
            num_scalar_prefetch=1,
            grid=(STEPS,),
            in_specs=[pl.BlockSpec((rows, width), lambda i, ids: (0, 0))],
            out_specs=pl.BlockSpec((block, width), lambda i, ids: (i, 0)),
            scratch_shapes=[
                pltpu.VMEM(((rows + 2) * parts, 128), F32),
                pltpu.VMEM((block * parts, 128), F32),
            ],
        ),
        compiler_params=params(56),
        name="gather_rows",
    )(ids, table)


def scatter_rows(ids, counts, grads, rows, owners, capacity):
    width = grads.shape[2]
    parts = 1 if width == 128 else 4
    sources = owners // STEPS if parts == 1 else 1
    return pl.pallas_call(
        scatter_kernel,
        out_shape=(jax.ShapeDtypeStruct((width // 2, rows), BF),) * 2,
        grid_spec=pltpu.PrefetchScalarGridSpec(
            num_scalar_prefetch=2,
            grid=(owners // sources,),
            in_specs=[pl.BlockSpec((sources, capacity, width), lambda i, *_: (i, 0, 0))],
            out_specs=(pl.BlockSpec((width // 2, rows), lambda i, *_: (0, 0)),) * 2,
            scratch_shapes=[
                pltpu.VMEM(((rows + 8) * parts, 128), F32),
                pltpu.VMEM((sources * capacity * parts, 128), F32),
            ],
        ),
        compiler_params=params(40),
        name="scatter_rows",
    )(ids, counts, grads)


def layer(place, arrived, slots, w_in, w_out, doc, og):
    events, width = og.shape
    wide = w_in.shape[1]
    first = (arrived.shape[0], width * 3 // 4)
    second = (arrived.shape[0], width // 4)
    vmem = pl.BlockSpec(memory_space=pltpu.VMEM)
    return pl.pallas_call(
        layer_kernel,
        in_specs=[pl.BlockSpec(memory_space=pltpu.SMEM)] + [vmem] * 6,
        out_shape=(
            jax.ShapeDtypeStruct((events, width), BF),
            jax.ShapeDtypeStruct(first, BF),
            jax.ShapeDtypeStruct(second, BF),
            jax.ShapeDtypeStruct((events, width), BF),
            jax.ShapeDtypeStruct((events, wide), BF),
            jax.ShapeDtypeStruct((events, width), BF),
        ),
        scratch_shapes=[
            pltpu.VMEM((events, width), BF),
            pltpu.VMEM((events, wide), BF),
            pltpu.VMEM((HEADS, events, events), BF),
            pltpu.VMEM((HEADS, events, events), BF),
            pltpu.VMEM((events, width), F32),
            pltpu.VMEM((events, width), BF),
            pltpu.VMEM((events, width), BF),
            pltpu.VMEM((events, 128), jnp.int32),
        ],
        compiler_params=params(60),
        name="layer",
    )(place, arrived, slots, w_in, w_out, doc, og)


def weight_grads(place, normed, du, gated, og):
    events, width = gated.shape
    steps = du.shape[1] // width
    whole = pl.BlockSpec((events, width), lambda c: (0, 0))
    part = pl.BlockSpec((width // 2, width), lambda c: (0, c))
    return pl.pallas_call(
        weights_kernel,
        grid=(steps + 1,),
        in_specs=[
            pl.BlockSpec(memory_space=pltpu.SMEM),
            whole,
            pl.BlockSpec((events, width), lambda c: (0, jnp.minimum(c, steps - 1))),
            whole,
            whole,
        ],
        out_specs=(part, part),
        out_shape=(jax.ShapeDtypeStruct((width // 2, du.shape[1] + width), BF),) * 2,
        scratch_shapes=[pltpu.VMEM((2, events, width), BF)],
        compiler_params=params(58),
        name="weight_grads",
    )(place, normed, du, gated, og)


def other_core(value):
    return lax.ppermute(value, "dp", [(d, d ^ 1) for d in range(8)])


def along_z(value, hop):
    return lax.ppermute(value, "dp", [(d, ((d // 2 + hop) % 4) * 2 + d % 2) for d in range(8)])


def ring_sum(pieces, move):
    half = pieces.shape[1] // 2
    far = pieces[2]
    ahead = move(far[:half], 1)
    behind = move(far[half:], -1)
    up = pieces[1].astype(F32)
    up = jnp.concatenate([up[:half] + ahead.astype(F32), up[half:]], axis=0).astype(BF)
    down = pieces[3].astype(F32)
    down = jnp.concatenate([down[:half], down[half:] + behind.astype(F32)], axis=0).astype(BF)
    return pieces[0].astype(F32) + move(up, 1).astype(F32) + move(down, -1).astype(F32)


def direct_sum(pieces, move):
    total = pieces[0].astype(F32)
    moved = [move(pieces[hop], hop) for hop in range(1, 4)]
    for value in moved:
        total = total + value.astype(F32)
    return total


def reduce_dp(value, along=ring_sum):
    keep, give = value
    mine = (keep.astype(F32) + other_core(give).astype(F32)).astype(BF)
    return along(mine.reshape((4, mine.shape[0] // 4) + mine.shape[1:]), along_z)


def whole(table, w_in, w_out, owner, local_row, doc_ids, out_grad):
    events, lookups_each = owner.shape
    rows_owned, width = table.shape
    owners = lax.axis_size("table")
    lookups = events * lookups_each
    capacity = 2 * lookups // owners
    wide = w_in.shape[1]
    slots, requests = route(owner.T, local_row.T, capacity, owners, rows_owned, width)
    asked = lax.all_to_all(requests, "table", split_axis=0, concat_axis=0, tiled=True)
    ids = asked.reshape(owners * capacity)
    counts = jnp.sum((asked < rows_owned * (width // 128)).astype(jnp.int32), axis=1)
    found = gather_rows(ids, table, owners, capacity)
    found = found.reshape(owners, capacity, width)
    arrived = lax.all_to_all(found, "table", split_axis=0, concat_axis=0, tiled=True)
    place = lax.axis_index("dp").astype(jnp.int32).reshape(1)
    layer_out, send_a, send_b, normed, du, gated = layer(
        place, arrived.reshape(owners * capacity, width), slots, w_in, w_out, doc_ids, out_grad
    )

    def exchange(value):
        return lax.all_to_all(value, "table", split_axis=0, concat_axis=0, tiled=True)

    def scatter(value):
        at = ids if value.shape[2] > 128 else ids // (width // 128)
        return scatter_rows(at, counts, value, rows_owned, owners, capacity)

    both = wide + width
    got_a = exchange(send_a.reshape(owners, capacity, -1))
    terms = weight_grads(place, normed, du, gated, out_grad)
    partial = reduce_dp(terms).astype(BF)
    lanes = width // 4
    parts = partial.reshape(owners, -1, lanes)
    got_b = exchange(
        jnp.concatenate([send_b.reshape(owners, capacity, lanes), parts], axis=1)
    )
    sum_a = scatter(got_a)
    mine = jnp.sum(got_b[:, capacity:].astype(F32), axis=0, keepdims=True).astype(BF)
    known = exchange(jnp.broadcast_to(mine, parts.shape))
    sum_b = scatter(got_b)
    known = known.reshape(width // 8, both)
    gathered = lax.all_gather(known, "dp", axis=0, tiled=True)
    grad_in, grad_out = finish(gathered, wide)
    mine_a = reduce_dp(sum_a)
    mine_b = reduce_dp(sum_b, direct_sum)
    mine = jnp.concatenate([mine_a, mine_b], axis=0)
    return (layer_out, grad_in, grad_out, mine.T)


def solution(mesh):
    placed = (
        P("table", None),
        P(),
        P(),
        P(("dp", "table"), None),
        P(("dp", "table"), None),
        P(("dp", "table"), None),
        P(("dp", "table"), None),
    )
    return jax.shard_map(
        whole,
        mesh=mesh,
        in_specs=placed,
        out_specs=(P(("dp", "table"), None), P(), P(), P("table", "dp")),
        check_vma=False,
    )
```

```python
import jax
import jax.numpy as jnp
from jax import lax
from jax.experimental import pallas as pl
from jax.experimental.pallas import tpu as pltpu
from jax.sharding import PartitionSpec as P


HEADS = 4
MAXLEN = 768
EPS = 1e-06
GROUP = 32
STEPS = 4
BF = jnp.bfloat16
F32 = jnp.float32
NN = (((1,), (0,)), ((), ()))
NT = (((1,), (1,)), ((), ()))
TN = (((0,), (0,)), ((), ()))


def dot(a, b, dims=NN):
    return lax.dot_general(a, b, dims, preferred_element_type=F32)


def iota(shape, dim):
    return lax.broadcasted_iota(jnp.int32, shape, dim)


def onehot(cond):
    return jnp.where(cond, 1.0, 0.0).astype(BF)


def route_kernel(own_ref, loc_ref, slot_ref, req_ref, *, owners, capacity, dummy, width):
    lanes = 128
    rows = slot_ref.shape[0]

    def stacked(ref):
        many, events = ref.shape
        return jnp.concatenate(
            [
                ref[j : j + 1, k : k + lanes]
                for j in range(many)
                for k in range(0, events, lanes)
            ],
            axis=0,
        )

    own = stacked(own_ref)
    loc = stacked(loc_ref)
    member = jnp.concatenate([onehot(own == o) for o in range(owners)], axis=0)
    total = owners * rows
    upper = onehot(iota((lanes, lanes), 0) <= iota((lanes, lanes), 1))
    inside = dot(member, upper)
    left = iota((total, total), 0)
    right = iota((total, total), 1)
    before = onehot((left // rows == right // rows) & (right < left))
    offset = jnp.sum(dot(before, member), axis=1, keepdims=True)
    place = (inside + offset - 1.0) * member.astype(F32)
    position = place[0:rows]
    for o in range(1, owners):
        position = position + place[o * rows : (o + 1) * rows]
    position = position.astype(jnp.int32)
    slot_ref[...] = own * capacity + position
    who = iota((owners, lanes), 0)
    where = iota((capacity, lanes), 0)
    found = jnp.zeros((3 * owners, capacity), F32)
    for r in range(rows):
        mine = own[r : r + 1, :] == who
        row = loc[r : r + 1, :]
        high = jnp.where(mine, (row >> 8).astype(F32), 0.0).astype(BF)
        low = jnp.where(mine, (row & 255).astype(F32), 0.0).astype(BF)
        left_side = jnp.concatenate([high, low, onehot(mine)], axis=0)
        found = found + dot(left_side, onehot(position[r : r + 1, :] == where), NT)
    high = found[0:owners].astype(jnp.int32)
    low = found[owners : 2 * owners].astype(jnp.int32)
    used = found[2 * owners :] > 0.5
    req_ref[...] = jnp.where(used, high * 256 + low, dummy) * (width // 128)


def gather_kernel(ids_ref, table_ref, out_ref, wide, picked):
    step = pl.program_id(0)
    count, width = out_ref.shape
    rows = table_ref.shape[0]
    parts = width // 128
    chunk = 64

    @pl.when(step == 0)
    def _():
        def widen(i, carry):
            base = pl.multiple_of(i * chunk, chunk)
            for c in range(parts):
                wide[pl.ds(base * parts + c, chunk, stride=parts), :] = table_ref[
                    pl.ds(base, chunk), c * 128 : (c + 1) * 128
                ].astype(F32)
            return carry

        lax.fori_loop(0, rows // chunk, widen, 0)
        wide[rows * parts : rows * parts + 8, :] = jnp.zeros((8, 128), F32)

    def copy_rows(k, carry):
        base = step * count + k * 16
        taken = k * (16 * parts)
        for u in range(16):
            row = ids_ref[base + u]
            picked[pl.ds(pl.multiple_of(taken + u * parts, parts), parts), :] = wide[
                pl.ds(pl.multiple_of(row, parts), parts), :
            ]
        return carry

    lax.fori_loop(0, count // 16, copy_rows, 0)
    for c in range(parts):
        out_ref[:, c * 128 : (c + 1) * 128] = picked[pl.ds(c, count, stride=parts), :].astype(BF)


def scatter_kernel(ids_ref, cnt_ref, grad_ref, keep_ref, give_ref, total, rows_in):
    step = pl.program_id(0)
    sources, count, width = grad_ref.shape
    used = width // 128
    half, rows = keep_ref.shape
    parts = rows_in.shape[0] // (sources * count)

    @pl.when(step == 0)
    def _():
        def clear(i, carry):
            total[pl.ds(pl.multiple_of(i * 256, 256), 256), :] = jnp.zeros((256, 128), F32)
            return carry

        lax.fori_loop(0, rows * parts // 256, clear, 0)

    for q in range(sources):
        for c in range(used):
            rows_in[pl.ds(q * count * parts + c, count, stride=parts), :] = grad_ref[
                q, :, c * 128 : (c + 1) * 128
            ].astype(F32)

    def add_rows(q, k):
        base = (step * sources + q) * count + k * GROUP
        taken = (q * count + k * GROUP) * parts
        for u in range(0, GROUP, 2):
            one = ids_ref[base + u]
            two = ids_ref[base + (u + 1)]
            first = pl.ds(pl.multiple_of(one, parts), parts)
            second = pl.ds(pl.multiple_of(two, parts), parts)
            left = rows_in[pl.ds(pl.multiple_of(taken + u * parts, parts), parts), :]
            right = rows_in[pl.ds(pl.multiple_of(taken + (u + 1) * parts, parts), parts), :]
            both = jnp.where(one == two, 1.0, 0.0)
            sum_one = total[first, :] + left
            sum_two = total[second, :] + (right + left * both)
            total[first, :] = sum_one
            total[second, :] = sum_two

    def add_source(q, carry):
        def group(k, inner):
            add_rows(q, k)
            return inner

        lax.fori_loop(0, (cnt_ref[step * sources + q] + (GROUP - 1)) // GROUP, group, 0)
        return carry

    lax.fori_loop(0, sources, add_source, 0)

    @pl.when(step == pl.num_programs(0) - 1)
    def _():
        def flush(i, carry):
            for c in range(used):
                block = total[pl.ds(i * (128 * parts) + c, 128, stride=parts), :].T.astype(BF)
                at = pl.ds(pl.multiple_of(i * 128, 128), 128)
                for q in range(2):
                    start = c * 128 + q * 64
                    out_ref = keep_ref if start < half else give_ref
                    out_ref[start % half : start % half + 64, at] = block[q * 64 : (q + 1) * 64]
            return carry

        lax.fori_loop(0, rows // 128, flush, 0)


def normal(values):
    center = values - jnp.mean(values, axis=-1, keepdims=True)
    spread = jnp.mean(center * center, axis=-1, keepdims=True)
    scale = lax.rsqrt(spread + EPS)
    return center * scale, scale


def normal_back(grad, unit, scale):
    shared = jnp.mean(grad, axis=-1, keepdims=True)
    along = jnp.mean(grad * unit, axis=-1, keepdims=True)
    return scale * (grad - shared - unit * along)


def spread_columns(place_ref, width, shares):
    column = iota((8, width), 1)
    place = place_ref[0]
    source = jnp.zeros((8, width), jnp.int32)
    start = 0
    for share in shares:
        inside = column - 8 * start
        piece = inside // share
        z = (place // 2 + piece) & 3
        core = (place + piece // 4) & 1
        here = (z * 2 + core) * (width // 8) + start + inside - piece * share
        source = jnp.where(inside >= 0, here, source)
        start += share
    return onehot(iota((width, width), 0) == source[0:1, :])


def layer_kernel(
    place_ref,
    arrived_ref,
    slot_ref,
    w_in_ref,
    w_out_ref,
    doc_ref,
    og_ref,
    out_ref,
    send_a_ref,
    send_b_ref,
    normed_ref,
    du_ref,
    gated_ref,
    emb_ref,
    proj_ref,
    wts_ref,
    dws_ref,
    mixed_ref,
    dmix_ref,
    eg_ref,
    col_ref,
):
    events, width = og_ref.shape
    slots = arrived_ref.shape[0]
    head = width // HEADS
    blk = 256
    nblk = events // blk
    lane_rows = events // 128
    cap_step = 256
    slot_all = slot_ref[...]
    slot_cols = slot_all.astype(F32).T.astype(jnp.int32)
    doc_rows = doc_ref[...]
    for r in range(lane_rows):
        rows = slice(r * 128, (r + 1) * 128)
        col_ref[rows, 0:1] = slot_cols[:, r : r + 1]
        col_ref[rows, 1:2] = slot_cols[:, lane_rows + r : lane_rows + r + 1]
    doc_cols = jnp.broadcast_to(doc_rows.astype(F32), (8, events)).T[:, 0:1].astype(jnp.int32)
    col_ref[:, 2:3] = doc_cols
    scale = head ** (-0.5)

    def steps(body, total, group):
        def several(k, carry):
            for u in range(group):
                body(k * group + u, carry)
            return carry

        if total == group:
            several(0, 0)
        else:
            lax.fori_loop(0, total // group, several, 0)

    def block_rows(b):
        return pl.ds(pl.multiple_of(b * blk, blk), blk)

    def unpack(b, carry):
        rows = block_rows(b)
        first = col_ref[rows, 0:1]
        second = col_ref[rows, 1:2]
        total = jnp.zeros((blk, width), F32)
        for o in range(slots // cap_step):
            where = iota((blk, cap_step), 1) + o * cap_step
            pick = onehot((where == first) | (where == second))
            total = total + dot(pick, arrived_ref[o * cap_step : (o + 1) * cap_step, :])
        embedded = total.astype(BF)
        emb_ref[rows, :] = embedded
        unit, _ = normal(embedded.astype(F32))
        normed = unit.astype(BF)
        normed_ref[rows, :] = normed
        for c in range(4):
            cols = slice(c * width, (c + 1) * width)
            u = dot(normed, w_in_ref[:, cols])
            sig = 0.5 * jnp.tanh(0.5 * u) + 0.5
            act = u * sig
            proj_ref[rows, cols] = act.astype(BF)
            du_ref[rows, cols] = (sig + act * (1.0 - sig)).astype(BF)
        return carry

    steps(unpack, nblk, 2)

    def heads_forward(h, carry):
        def cols(part):
            return pl.ds(pl.multiple_of(part * width + h * head, head), head)

        mine = pl.ds(pl.multiple_of(h * head, head), head)
        for i in range(nblk):
            rows = slice(i * blk, (i + 1) * blk)
            query = proj_ref[rows, cols(2)]
            total = jnp.zeros((blk, head), F32)
            for j in range(i + 1):
                keys = slice(j * blk, (j + 1) * blk)
                scores = dot(query, proj_ref[keys, cols(3)], NT) * scale
                allowed = col_ref[rows, 2:3] == doc_rows[:, keys]
                if i == j:
                    allowed = allowed & (iota((blk, blk), 0) >= iota((blk, blk), 1))
                sig = 0.5 * jnp.tanh(0.5 * scores) + 0.5
                act = scores * sig
                weight = jnp.where(allowed, act * (1.0 / MAXLEN), 0.0).astype(BF)
                slope = sig + act * (1.0 - sig)
                wts_ref[h, rows, keys] = weight
                dws_ref[h, rows, keys] = jnp.where(allowed, slope * (scale / MAXLEN), 0.0).astype(BF)
                total = total + dot(weight, proj_ref[keys, cols(1)])
            mixed_ref[rows, mine] = total
        return carry

    lax.fori_loop(0, HEADS, heads_forward, 0)

    def middle(b, carry):
        rows = block_rows(b)
        unit, spread = normal(mixed_ref[rows, :])
        gate = proj_ref[rows, 0:width].astype(F32)
        gated = (unit * gate).astype(BF)
        gated_ref[rows, :] = gated
        out_ref[rows, :] = (emb_ref[rows, :].astype(F32) + dot(gated, w_out_ref[...])).astype(BF)
        dgated = dot(og_ref[rows, :], w_out_ref[...], NT).astype(BF).astype(F32)
        dmix_ref[rows, :] = normal_back(dgated * gate, unit, spread).astype(BF)
        dgate = (dgated * unit).astype(BF).astype(F32)
        du_ref[rows, 0:width] = (dgate * du_ref[rows, 0:width].astype(F32)).astype(BF)
        return carry

    steps(middle, nblk, 1)

    def heads_backward(h, carry):
        def cols(part):
            return pl.ds(pl.multiple_of(part * width + h * head, head), head)

        mine = pl.ds(pl.multiple_of(h * head, head), head)

        def put(rows, part, value):
            at = cols(part)
            du_ref[rows, at] = (
                value.astype(BF).astype(F32) * du_ref[rows, at].astype(F32)
            ).astype(BF)

        for j in range(nblk):
            keys = slice(j * blk, (j + 1) * blk)
            value = proj_ref[keys, cols(1)]
            dkey = jnp.zeros((blk, head), F32)
            dvalue = jnp.zeros((blk, head), F32)
            for i in range(j, nblk):
                rows = slice(i * blk, (i + 1) * blk)
                dmix = dmix_ref[rows, mine]
                dscore = (
                    dot(dmix, value, NT) * dws_ref[h, rows, keys].astype(F32)
                ).astype(BF)
                dws_ref[h, rows, keys] = dscore
                dvalue = dvalue + dot(wts_ref[h, rows, keys], dmix, TN)
                dkey = dkey + dot(dscore, proj_ref[rows, cols(2)], TN)
            put(keys, 1, dvalue)
            put(keys, 3, dkey)
        for i in range(nblk):
            rows = slice(i * blk, (i + 1) * blk)
            upto = slice(0, (i + 1) * blk)
            put(rows, 2, dot(dws_ref[h, rows, upto], proj_ref[upto, cols(3)]))
        return carry

    lax.fori_loop(0, HEADS, heads_backward, 0)

    spread = spread_columns(place_ref, width, (send_a_ref.shape[1] // 8, send_b_ref.shape[1] // 8))

    def last(b, carry):
        rows = block_rows(b)
        dnormed = dot(du_ref[rows, :], w_in_ref[...], NT).astype(BF).astype(F32)
        unit, size = normal(emb_ref[rows, :].astype(F32))
        grad = normal_back(dnormed, unit, size) + og_ref[rows, :].astype(F32)
        eg_ref[rows, :] = dot(grad.astype(BF), spread).astype(BF)
        return carry

    steps(last, nblk, 2)

    def pack(o, carry):
        where = iota((cap_step, 128), 0) + o * cap_step
        picks = [
            onehot(
                (where == slot_all[r : r + 1, :])
                | (where == slot_all[lane_rows + r : lane_rows + r + 1, :])
            )
            for r in range(lane_rows)
        ]
        packed = dot(jnp.concatenate(picks, axis=1), eg_ref[...]).astype(BF)
        at = pl.ds(pl.multiple_of(o * cap_step, cap_step), cap_step)
        send_a_ref[at, :] = packed[:, : send_a_ref.shape[1]]
        send_b_ref[at, :] = packed[:, send_a_ref.shape[1] :]
        return carry

    steps(pack, slots // cap_step, 16)


def weights_kernel(place_ref, normed_ref, du_ref, gated_ref, og_ref, keep_ref, give_ref, turned):
    step = pl.program_id(0)
    last = pl.num_programs(0) - 1
    width = gated_ref.shape[1]
    half = width // 2

    @pl.when(step == 0)
    def _():
        spread = spread_columns(place_ref, width, (width // 8,))
        turned[0] = dot(normed_ref[...], spread).astype(BF)
        turned[1] = dot(gated_ref[...], spread).astype(BF)

    def put(value):
        keep_ref[...] = value[:half].astype(BF)
        give_ref[...] = value[half:].astype(BF)

    @pl.when(step < last)
    def _():
        put(dot(turned[0], du_ref[...], TN))

    @pl.when(step == last)
    def _():
        put(dot(turned[1], og_ref[...], TN))


def finish_kernel(sum_ref, first_ref, second_ref):
    wide = first_ref.shape[1]
    first_ref[...] = sum_ref[:, :wide].astype(F32)
    second_ref[...] = sum_ref[:, wide:].astype(F32)


def params(mib, **more):
    return pltpu.CompilerParams(vmem_limit_bytes=mib * 2**20, **more)


def route(own, loc, capacity, owners, dummy, width):
    return pl.pallas_call(
        lambda *refs: route_kernel(*refs, owners=owners, capacity=capacity, dummy=dummy, width=width),
        out_shape=(
            jax.ShapeDtypeStruct((own.size // 128, 128), jnp.int32),
            jax.ShapeDtypeStruct((owners, capacity), jnp.int32),
        ),
        name="route",
    )(own, loc)


def finish(summed, wide):
    rows, both = summed.shape
    return pl.pallas_call(
        finish_kernel,
        out_shape=(
            jax.ShapeDtypeStruct((rows, wide), F32),
            jax.ShapeDtypeStruct((rows, both - wide), F32),
        ),
        grid=(8,),
        in_specs=[pl.BlockSpec((rows // 8, both), lambda i: (i, 0))],
        out_specs=(
            pl.BlockSpec((rows // 8, wide), lambda i: (i, 0)),
            pl.BlockSpec((rows // 8, both - wide), lambda i: (i, 0)),
        ),
        compiler_params=params(16),
        name="finish",
    )(summed)


def gather_rows(ids, table, owners, capacity):
    rows, width = table.shape
    parts = width // 128
    block = owners * capacity // STEPS
    return pl.pallas_call(
        gather_kernel,
        out_shape=jax.ShapeDtypeStruct((owners * capacity, width), BF),
        grid_spec=pltpu.PrefetchScalarGridSpec(
            num_scalar_prefetch=1,
            grid=(STEPS,),
            in_specs=[pl.BlockSpec((rows, width), lambda i, ids: (0, 0))],
            out_specs=pl.BlockSpec((block, width), lambda i, ids: (i, 0)),
            scratch_shapes=[
                pltpu.VMEM(((rows + 2) * parts, 128), F32),
                pltpu.VMEM((block * parts, 128), F32),
            ],
        ),
        compiler_params=params(56),
        name="gather_rows",
    )(ids, table)


def scatter_rows(ids, counts, grads, rows, owners, capacity):
    width = grads.shape[2]
    parts = 1 if width == 128 else 4
    sources = owners // STEPS if parts == 1 else 1
    return pl.pallas_call(
        scatter_kernel,
        out_shape=(jax.ShapeDtypeStruct((width // 2, rows), BF),) * 2,
        grid_spec=pltpu.PrefetchScalarGridSpec(
            num_scalar_prefetch=2,
            grid=(owners // sources,),
            in_specs=[pl.BlockSpec((sources, capacity, width), lambda i, *_: (i, 0, 0))],
            out_specs=(pl.BlockSpec((width // 2, rows), lambda i, *_: (0, 0)),) * 2,
            scratch_shapes=[
                pltpu.VMEM(((rows + 8) * parts, 128), F32),
                pltpu.VMEM((sources * capacity * parts, 128), F32),
            ],
        ),
        compiler_params=params(40),
        name="scatter_rows",
    )(ids, counts, grads)


def layer(place, arrived, slots, w_in, w_out, doc, og):
    events, width = og.shape
    wide = w_in.shape[1]
    first = (arrived.shape[0], width * 3 // 4)
    second = (arrived.shape[0], width // 4)
    vmem = pl.BlockSpec(memory_space=pltpu.VMEM)
    return pl.pallas_call(
        layer_kernel,
        in_specs=[pl.BlockSpec(memory_space=pltpu.SMEM)] + [vmem] * 6,
        out_shape=(
            jax.ShapeDtypeStruct((events, width), BF),
            jax.ShapeDtypeStruct(first, BF),
            jax.ShapeDtypeStruct(second, BF),
            jax.ShapeDtypeStruct((events, width), BF),
            jax.ShapeDtypeStruct((events, wide), BF),
            jax.ShapeDtypeStruct((events, width), BF),
        ),
        scratch_shapes=[
            pltpu.VMEM((events, width), BF),
            pltpu.VMEM((events, wide), BF),
            pltpu.VMEM((HEADS, events, events), BF),
            pltpu.VMEM((HEADS, events, events), BF),
            pltpu.VMEM((events, width), F32),
            pltpu.VMEM((events, width), BF),
            pltpu.VMEM((events, width), BF),
            pltpu.VMEM((events, 128), jnp.int32),
        ],
        compiler_params=params(60),
        name="layer",
    )(place, arrived, slots, w_in, w_out, doc, og)


def weight_grads(place, normed, du, gated, og):
    events, width = gated.shape
    steps = du.shape[1] // width
    whole = pl.BlockSpec((events, width), lambda c: (0, 0))
    part = pl.BlockSpec((width // 2, width), lambda c: (0, c))
    return pl.pallas_call(
        weights_kernel,
        grid=(steps + 1,),
        in_specs=[
            pl.BlockSpec(memory_space=pltpu.SMEM),
            whole,
            pl.BlockSpec((events, width), lambda c: (0, jnp.minimum(c, steps - 1))),
            whole,
            whole,
        ],
        out_specs=(part, part),
        out_shape=(jax.ShapeDtypeStruct((width // 2, du.shape[1] + width), BF),) * 2,
        scratch_shapes=[pltpu.VMEM((2, events, width), BF)],
        compiler_params=params(58),
        name="weight_grads",
    )(place, normed, du, gated, og)


def other_core(value):
    return lax.ppermute(value, "dp", [(d, d ^ 1) for d in range(8)])


def along_z(value, hop):
    return lax.ppermute(value, "dp", [(d, ((d // 2 + hop) % 4) * 2 + d % 2) for d in range(8)])


def ring_sum(pieces, move):
    half = pieces.shape[1] // 2
    far = pieces[2]
    ahead = move(far[:half], 1)
    behind = move(far[half:], -1)
    up = pieces[1].astype(F32)
    up = jnp.concatenate([up[:half] + ahead.astype(F32), up[half:]], axis=0).astype(BF)
    down = pieces[3].astype(F32)
    down = jnp.concatenate([down[:half], down[half:] + behind.astype(F32)], axis=0).astype(BF)
    from_up = move(up, 1)
    from_down = move(down, -1)
    return pieces[0].astype(F32) + from_up.astype(F32) + from_down.astype(F32)


def direct_sum(pieces, move):
    total = pieces[0].astype(F32)
    moved = [move(pieces[hop], hop) for hop in range(1, 4)]
    for value in moved:
        total = total + value.astype(F32)
    return total


def reduce_dp(value, along=ring_sum):
    keep, give = value
    mine = (keep.astype(F32) + other_core(give).astype(F32)).astype(BF)
    return along(mine.reshape((4, mine.shape[0] // 4) + mine.shape[1:]), along_z)


def whole(table, w_in, w_out, owner, local_row, doc_ids, out_grad):
    events, lookups_each = owner.shape
    rows_owned, width = table.shape
    owners = lax.axis_size("table")
    lookups = events * lookups_each
    capacity = 2 * lookups // owners
    wide = w_in.shape[1]
    slots, requests = route(owner.T, local_row.T, capacity, owners, rows_owned, width)
    asked = lax.all_to_all(requests, "table", split_axis=0, concat_axis=0, tiled=True)
    ids = asked.reshape(owners * capacity)
    counts = jnp.sum((asked < rows_owned * (width // 128)).astype(jnp.int32), axis=1)
    found = gather_rows(ids, table, owners, capacity)
    found = found.reshape(owners, capacity, width)
    arrived = lax.all_to_all(found, "table", split_axis=0, concat_axis=0, tiled=True)
    place = lax.axis_index("dp").astype(jnp.int32).reshape(1)
    layer_out, send_a, send_b, normed, du, gated = layer(
        place, arrived.reshape(owners * capacity, width), slots, w_in, w_out, doc_ids, out_grad
    )

    def exchange(value):
        return lax.all_to_all(value, "table", split_axis=0, concat_axis=0, tiled=True)

    def scatter(value):
        at = ids if value.shape[2] > 128 else ids // (width // 128)
        return scatter_rows(at, counts, value, rows_owned, owners, capacity)

    both = wide + width
    got_a = exchange(send_a.reshape(owners, capacity, -1))
    terms = weight_grads(place, normed, du, gated, out_grad)
    partial = reduce_dp(terms).astype(BF)
    lanes = width // 4
    parts = partial.reshape(owners, -1, lanes)
    got_b = exchange(
        jnp.concatenate([send_b.reshape(owners, capacity, lanes), parts], axis=1)
    )
    sum_a = scatter(got_a)
    mine = jnp.sum(got_b[:, capacity:].astype(F32), axis=0, keepdims=True).astype(BF)
    known = exchange(jnp.broadcast_to(mine, parts.shape))
    sum_b = scatter(got_b)
    known = known.reshape(width // 8, both)
    gathered = lax.all_gather(known, "dp", axis=0, tiled=True)
    grad_in, grad_out = finish(gathered, wide)
    mine_a = reduce_dp(sum_a)
    mine_b = reduce_dp(sum_b, direct_sum)
    mine = jnp.concatenate([mine_a, mine_b], axis=0)
    return (layer_out, grad_in, grad_out, mine.T)


def solution(mesh):
    placed = (
        P("table", None),
        P(),
        P(),
        P(("dp", "table"), None),
        P(("dp", "table"), None),
        P(("dp", "table"), None),
        P(("dp", "table"), None),
    )
    return jax.shard_map(
        whole,
        mesh=mesh,
        in_specs=placed,
        out_specs=(P(("dp", "table"), None), P(), P(), P("table", "dp")),
        check_vma=False,
    )
```
